32 devices in a mesh: tilt: 2 (over y), row: 8 (over z, x), col: 2 (over core).
Axes of the slice: x: 2, y: 2, z: 4, core: 2. Of those that a mesh axis runs over, the one named last changes fastest.
Arguments:
- object_field: float32 [2, 2048, 256], P(None, ('tilt', 'row'), 'col'), parts along dimension 1, may hold values from -4.2 to 4.2
- probe: float32 [8, 2, 128, 128], P('tilt'), parts along dimension 0, may hold values from -2.1 to 2.1
- patterns: float32 [16, 2, 2, 128, 128], P(('tilt', 'row'), 'col'), parts along dimension 0, may hold values from 0.1 to 3
- offsets: int32 [16, 2, 2, 2], P(('tilt', 'row'), 'col'), parts along dimension 0, may hold values from 0 to 256
- counts: int32 [16, 2], P(('tilt', 'row'), 'col'), parts along dimension 0, may hold values from 1 to 2, as said below
Outputs:
- object_out: float32 [2, 2048, 256], P(None, ('tilt', 'row'), 'col'), parts along dimension 1
- probe_out: float32 [8, 2, 128, 128], P('tilt'), parts along dimension 0
The draws below stay inside these ranges and needn't reach their ends.
There are 2 independent parts, one for each index of `tilt`. The reference program is written for one: setup_inputs(seed, part) draws one part's arguments, and reference() takes and returns one part's arrays. A program takes and returns all parts, laid end to end along the dimension named above; each array names one. Nothing has to cross between parts.
Inputs may be any that keep to these rules, and one draw needn't show every extreme that they name: Only the first counts[r, c] slots of a tile are live; some tile has all 2 live. `offsets`: A window lies inside its tile's frame of 384 pixels a side.
All inputs are finite; a program needn't handle non-finite values.
Results may differ from the reference program's by a relative error of at most 0.0003.
Values sent between devices are 32-bit elements; how exact they have to be, the bound alone decides.
No kernel may reach another device: no remote copies, remote signals or barrier semaphores. Data moves between devices by JAX's collectives and lax.ppermute only.
A program may use at most 64 MiB of HBM per device.

```python
import math
import jax
import jax.numpy as jnp
from jax import lax

B = 128
H = 128
P_SIZE = 128
MODES = 4
POS = 2
ITERS = 1
TILE_ROWS = 8
TILE_COLS = 2
NY = 1024
NX = 256


def draw_counts(key, part):
    light_key = jax.random.fold_in(key, 101)
    busy_key = jax.random.fold_in(key, 202)
    chosen_key = jax.random.fold_in(key, 303)
    light_tiles = jax.random.randint(light_key, (TILE_ROWS, TILE_COLS), 1, max(POS // 2, 1) + 1)
    busy_tiles = jax.random.randint(busy_key, (TILE_ROWS, TILE_COLS), 0, 8) == 0
    filled = jnp.where(busy_tiles, POS, light_tiles).reshape(-1)
    chosen_tile = jax.random.randint(chosen_key, (), 0, TILE_ROWS * TILE_COLS)
    filled = filled.at[chosen_tile].set(POS)
    return filled.reshape(TILE_ROWS, TILE_COLS).astype(jnp.int32)


def plant(result, rng, least, top_value):
    shape = result.shape
    spot = [jax.random.randint(jax.random.fold_in(rng, axis), (), 0, shape[axis]) for axis in range(len(shape))]
    result = result.at[tuple(spot)].set(least)
    longest = shape.index(max(shape))
    spot[longest] = (spot[longest] + 1) % shape[longest]
    return result.at[tuple(spot)].set(top_value)


def steps_of(rng, shape, shards, least, top_value):
    def one(dim, blocks):
        draws = jax.random.uniform(jax.random.fold_in(jax.random.fold_in(rng, 6), dim), (blocks,), jnp.float32, least / len(shards), top_value / len(shards))
        return jnp.repeat(jnp.exp(draws), shape[dim] // blocks).reshape((-1,) + (1,) * (len(shape) - dim - 1))

    factor_of = one(*shards[0])
    for cut in shards[1:]:
        factor_of = factor_of * one(*cut)
    return factor_of


def scatter_about(key, dims, spread, most, cuts=(), kind=jnp.bfloat16):
    entries = spread * jax.random.normal(key, dims, jnp.float32)
    if cuts:
        entries = entries * steps_of(key, dims, cuts, -0.22, 0.18)
    return jnp.clip(entries, -most, most).astype(kind)


def setup_inputs(seed: int = 0, part: int = 0) -> dict:
    keys = jax.random.split(jax.random.key(seed), 6)
    part_keys = jax.random.split(jax.random.fold_in(keys[5], part), 6)
    object_field = scatter_about(part_keys[0], (2, NY, NX), 0.7, 4.2, ((1, 8), (2, 2)), jnp.float32)
    probe = scatter_about(part_keys[1], (MODES, 2, P_SIZE, P_SIZE), 0.35, 2.1, (), jnp.float32)
    patterns = jnp.clip(jnp.exp(math.log(3.0) - 3.4011974 * jax.random.uniform(part_keys[2], (TILE_ROWS, TILE_COLS, POS, P_SIZE, P_SIZE), jnp.float32) ** steps_of(part_keys[2], (TILE_ROWS, TILE_COLS, POS, P_SIZE, P_SIZE), ((0, 8), (1, 2)), -0.2, 0.2)), 0.1, 3.0)
    offsets = plant(jax.random.randint(part_keys[3], (TILE_ROWS, TILE_COLS, POS, 2), 0, B + 2 * H - P_SIZE + 1), jax.random.fold_in(part_keys[3], 1), 0, B + 2 * H - P_SIZE).astype(jnp.int32)
    counts = draw_counts(jax.random.fold_in(jax.random.fold_in(keys[5], part), 71), part)
    return dict(object_field=object_field, probe=probe, patterns=patterns, offsets=offsets, counts=counts)


object_rate = 1.0
probe_rate = 1.0
epsilon = 1e-06

def as_index(value):
    return jnp.asarray(value).astype(jnp.int32)

def dft_tables(length):
    counter = jnp.arange(length, dtype=jnp.int32)
    product = counter[:, None] * counter[None, :] % length
    angle = -2.0 * jnp.pi / length * product.astype(jnp.float32)
    norm = 1.0 / jnp.sqrt(jnp.float32(length))
    return (jnp.cos(angle) * norm, jnp.sin(angle) * norm)

def left_product(cos_table, sin_table, real_part, imag_part):
    hp = lax.Precision.HIGHEST
    real_out = jnp.einsum('ab,kbc->kac', cos_table, real_part, precision=hp) - jnp.einsum('ab,kbc->kac', sin_table, imag_part, precision=hp)
    imag_out = jnp.einsum('ab,kbc->kac', cos_table, imag_part, precision=hp) + jnp.einsum('ab,kbc->kac', sin_table, real_part, precision=hp)
    return (real_out, imag_out)

def right_product(real_part, imag_part, cos_table, sin_table):
    hp = lax.Precision.HIGHEST
    real_out = jnp.einsum('kab,bc->kac', real_part, cos_table, precision=hp) - jnp.einsum('kab,bc->kac', imag_part, sin_table, precision=hp)
    imag_out = jnp.einsum('kab,bc->kac', real_part, sin_table, precision=hp) + jnp.einsum('kab,bc->kac', imag_part, cos_table, precision=hp)
    return (real_out, imag_out)

def transform(real_part, imag_part, cos_table, sin_table):
    middle_re, middle_im = left_product(cos_table, sin_table, real_part, imag_part)
    return right_product(middle_re, middle_im, cos_table, sin_table)

def slot_terms(window, probe, pattern, cos_table, sin_table):
    window_re, window_im = (window[0], window[1])
    probe_re, probe_im = (probe[:, 0], probe[:, 1])
    exit_re = probe_re * window_re - probe_im * window_im
    exit_im = probe_re * window_im + probe_im * window_re
    far_re, far_im = transform(exit_re, exit_im, cos_table, sin_table)
    intensity = lax.optimization_barrier(jnp.sum(far_re * far_re + far_im * far_im, axis=0))
    misfit = intensity - pattern
    back_re, back_im = transform(misfit * far_re, misfit * far_im, cos_table, -sin_table)
    grad_re = lax.optimization_barrier(jnp.sum(probe_re * back_re + probe_im * back_im, axis=0))
    grad_im = lax.optimization_barrier(jnp.sum(probe_re * back_im - probe_im * back_re, axis=0))
    term_re = window_re * back_re + window_im * back_im
    term_im = window_re * back_im - window_im * back_re
    return (jnp.stack([grad_re, grad_im]), jnp.stack([term_re, term_im], axis=1))

def reference(object_field, probe, patterns, offsets, counts):
    cos_table, sin_table = dft_tables(P_SIZE)
    frame_size = B + 2 * H
    for iteration in range(ITERS):
        padded = jnp.pad(object_field, ((0, 0), (H, H), (H, H)))

        def tile_step(carry, tile_index):
            gradient, probe_grad = carry
            tile_row = as_index(tile_index // TILE_COLS)
            tile_col = as_index(tile_index % TILE_COLS)
            frame = lax.dynamic_slice(padded, (as_index(0), tile_row * B, tile_col * B), (2, frame_size, frame_size))

            def slot_step(slot_index, inner):
                local_grad, probe_acc = inner
                slot_index = as_index(slot_index)
                corner_y = as_index(offsets[tile_row, tile_col, slot_index, 0])
                corner_x = as_index(offsets[tile_row, tile_col, slot_index, 1])
                window = lax.dynamic_slice(frame, (as_index(0), corner_y, corner_x), (2, P_SIZE, P_SIZE))
                window_grad, probe_term = slot_terms(window, probe, patterns[tile_row, tile_col, slot_index], cos_table, sin_table)
                live = (slot_index < counts[tile_row, tile_col]).astype(jnp.float32)
                region = lax.dynamic_slice(local_grad, (as_index(0), corner_y, corner_x), (2, P_SIZE, P_SIZE)) + live * window_grad
                local_grad = lax.dynamic_update_slice(local_grad, region, (as_index(0), corner_y, corner_x))
                return (local_grad, probe_acc + live * probe_term)
            local_grad = jnp.zeros((2, frame_size, frame_size), jnp.float32)
            local_grad, probe_grad = lax.fori_loop(0, POS, slot_step, (local_grad, probe_grad))
            start = (as_index(0), tile_row * B, tile_col * B)
            region = lax.dynamic_slice(gradient, start, (2, frame_size, frame_size)) + local_grad
            gradient = lax.dynamic_update_slice(gradient, region, start)
            return ((gradient, probe_grad), None)
        start_carry = (jnp.zeros_like(padded), jnp.zeros_like(probe))
        (gradient, probe_grad), unused = lax.scan(tile_step, start_carry, jnp.arange(TILE_ROWS * TILE_COLS, dtype=jnp.int32))
        object_grad = gradient[:, H:H + NY, H:H + NX]
        weight = jnp.max(lax.optimization_barrier(jnp.sum(probe[:, 0] * probe[:, 0] + probe[:, 1] * probe[:, 1], axis=0))) + epsilon
        object_field = object_field - object_rate * object_grad / weight
        probe = probe - probe_rate * probe_grad / (TILE_ROWS * TILE_COLS)
    return (object_field, probe)
```

```python
import jax
import jax.numpy as jnp
import numpy as np
from jax import lax
from jax.experimental import pallas as pl
from jax.experimental.pallas import tpu as pltpu
from jax.sharding import PartitionSpec as P

H = 128


object_rate = 1.0
probe_rate = 1.0
epsilon = 1e-06


def split(value):
    high = value.astype(jnp.bfloat16)
    low = (value - high.astype(jnp.float32)).astype(jnp.bfloat16)
    return high, low


def host_tables(length):
    counter = np.arange(length)
    angle = -2.0 * np.pi / length * (counter[:, None] * counter[None, :] % length)
    cosine = (np.cos(angle) / np.sqrt(length)).astype(np.float32)
    sine = (np.sin(angle) / np.sqrt(length)).astype(np.float32)
    plain = np.block([[cosine, sine], [-sine, cosine]])
    conj = np.block([[cosine, -sine], [sine, cosine]])
    both = np.stack([plain, conj])
    high = both.astype(jnp.bfloat16)
    low = (both - high.astype(np.float32)).astype(jnp.bfloat16)
    return np.concatenate([high, low])


def slots_kernel(
    place_ref,
    offsets_ref,
    counts_ref,
    own_ref,
    own_pair_ref,
    near_ref,
    near_pair_ref,
    far_ref,
    far_pair_ref,
    probe_ref,
    patterns_ref,
    tables_ref,
    keep_probe_ref,
    send_probe_ref,
    keep_grad_ref,
    send_grad_ref,
    weight_ref,
    frame,
    grad,
    term,
):
    modes = probe_ref.shape[0]
    width = probe_ref.shape[-1]
    slots = patterns_ref.shape[2]
    half = modes // 2
    core = place_ref[0]
    odd = place_ref[1]
    near_at = pl.multiple_of((1 - odd) * (2 * width), width)
    far_at = pl.multiple_of(odd * (2 * width), width)
    pair_at = 2 - 2 * core
    void_at = 2 * core

    empty = jnp.zeros((2, 3 * width, width), jnp.float32)
    frame[3] = empty
    frame[void_at] = empty
    frame[1, :, pl.ds(width, width), :] = own_ref[...]
    frame[1, :, pl.ds(near_at, width), :] = near_ref[...]
    frame[1, :, pl.ds(far_at, width), :] = far_ref[...]
    frame[pair_at, :, pl.ds(width, width), :] = own_pair_ref[...]
    frame[pair_at, :, pl.ds(near_at, width), :] = near_pair_ref[...]
    frame[pair_at, :, pl.ds(far_at, width), :] = far_pair_ref[...]
    grad[...] = jnp.zeros_like(grad)

    power = jnp.zeros((width, width), jnp.float32)
    for k in range(modes):
        power = power + probe_ref[k, 0] * probe_ref[k, 0] + probe_ref[k, 1] * probe_ref[k, 1]
    weight_ref[...] = jnp.full(weight_ref.shape, jnp.max(power) + epsilon, jnp.float32)

    lane = lax.broadcasted_iota(jnp.int32, (width, width), 1)

    def right(parts, which):
        value = jnp.concatenate([jnp.concatenate(part, axis=1) for part in parts], axis=0)
        high, low = split(value)
        table = jnp.concatenate(
            [tables_ref[which], tables_ref[which], tables_ref[2 + which]], axis=0
        )
        out = jnp.dot(
            jnp.concatenate([high, low, high], axis=1), table, preferred_element_type=jnp.float32
        )
        return [
            (out[k * width : (k + 1) * width, :width], out[k * width : (k + 1) * width, width:])
            for k in range(modes)
        ]

    def left(parts, which):
        value = jnp.concatenate([jnp.concatenate(part, axis=0) for part in parts], axis=1)
        high, low = split(value)
        table = jnp.concatenate(
            [tables_ref[1 - which], tables_ref[3 - which], tables_ref[1 - which]], axis=1
        )
        out = jnp.dot(
            table, jnp.concatenate([high, high, low], axis=0), preferred_element_type=jnp.float32
        )
        return [
            (out[:width, k * width : (k + 1) * width], out[width:, k * width : (k + 1) * width])
            for k in range(modes)
        ]

    for slot in range(slots):
        corner_y = offsets_ref[0, 0, slot, 0]
        corner_x = offsets_ref[0, 0, slot, 1]
        column = corner_x // width
        shift = corner_x - column * width
        back_shift = lax.rem(width - shift, width)
        rows = pl.ds(corner_y, width)
        live = (slot < counts_ref[0, 0]).astype(jnp.float32)

        window = []
        for part in range(2):
            both = jnp.where(
                lane >= shift, frame[column, part, rows, :], frame[column + 1, part, rows, :]
            )
            window.append(pltpu.roll(both, back_shift, 1))
        win_re, win_im = window

        exits = []
        for k in range(modes):
            probe_re, probe_im = probe_ref[k, 0], probe_ref[k, 1]
            exits.append(
                (
                    probe_re * win_re - probe_im * win_im,
                    probe_re * win_im + probe_im * win_re,
                )
            )
        far = left(right(exits, 0), 0)
        intensity = sum(re * re + im * im for re, im in far)
        misfit = (intensity - patterns_ref[0, 0, slot]) * live
        back = right(left([(misfit * re, misfit * im) for re, im in far], 1), 1)

        grad_re = jnp.zeros((width, width), jnp.float32)
        grad_im = jnp.zeros((width, width), jnp.float32)
        for k in range(modes):
            probe_re, probe_im = probe_ref[k, 0], probe_ref[k, 1]
            back_re, back_im = back[k]
            grad_re = grad_re + probe_re * back_re + probe_im * back_im
            grad_im = grad_im + probe_re * back_im - probe_im * back_re
            term_re = win_re * back_re + win_im * back_im
            term_im = win_re * back_im - win_im * back_re
            if slot == 0:
                term[k, 0] = term_re
                term[k, 1] = term_im
            else:
                term[k, 0] += term_re
                term[k, 1] += term_im
        for part, value in enumerate((grad_re, grad_im)):
            turned = pltpu.roll(value, shift, 1)
            grad[column, part, rows, :] += jnp.where(lane >= shift, turned, 0.0)
            grad[column + 1, part, rows, :] += jnp.where(lane >= shift, 0.0, turned)

    mine = core * half
    theirs = half - mine
    keep_probe_ref[...] = term[pl.ds(mine, half)]
    send_probe_ref[...] = term[pl.ds(theirs, half)]
    for index, place in enumerate((near_at, far_at, width)):
        keep_grad_ref[index] = grad[1, :, pl.ds(place, width), :]
        send_grad_ref[index] = grad[pair_at, :, pl.ds(place, width), :]


def run_slots(place, offsets, counts, blocks, probe, patterns):
    modes, _, width, _ = probe.shape
    half = modes // 2
    tables = jnp.asarray(host_tables(width))
    smem = pl.BlockSpec(memory_space=pltpu.SMEM)
    vmem = pl.BlockSpec(memory_space=pltpu.VMEM)
    probe_half = jax.ShapeDtypeStruct((half, 2, width, width), jnp.float32)
    grad_rows = jax.ShapeDtypeStruct((3, 2, width, width), jnp.float32)
    slots = patterns.shape[2]
    return pl.pallas_call(
        slots_kernel,
        out_shape=(
            probe_half,
            probe_half,
            grad_rows,
            grad_rows,
            jax.ShapeDtypeStruct((8, width), jnp.float32),
        ),
        in_specs=[smem] * 3 + [vmem] * 9,
        out_specs=(vmem,) * 5,
        scratch_shapes=[
            pltpu.VMEM((4, 2, 3 * width, width), jnp.float32),
            pltpu.VMEM((4, 2, 3 * width, width), jnp.float32),
            pltpu.VMEM((modes, 2, width, width), jnp.float32),
        ],
        cost_estimate=pl.CostEstimate(
            flops=slots * modes * 4 * 3 * 8 * width**3,
            bytes_accessed=40 * width * width * 4,
            transcendentals=0,
        ),
        name="slots",
    )(place, offsets, counts, *blocks, probe, patterns, tables)


def body(object_field, probe, patterns, offsets, counts):
    row_total = lax.axis_size("row")
    tile_total = row_total * lax.axis_size("col")
    modes, _, width, _ = probe.shape
    half = modes // 2
    row = lax.axis_index("row")
    core = lax.axis_index("col")
    place = jnp.stack([core, row % 2]).astype(jnp.int32)

    pair = [(0, 1), (1, 0)]
    near = [(i, i ^ 1) for i in range(row_total)]
    far = [(i, i + 1) for i in range(1, row_total - 1, 2)]
    far = far + [(target, source) for source, target in far]

    near_block = lax.ppermute(object_field, "row", near)
    far_block = lax.ppermute(object_field, "row", far)
    own_pair = lax.ppermute(object_field, "col", pair)
    near_pair = lax.ppermute(near_block, "col", pair)
    far_pair = lax.ppermute(far_block, "col", pair)
    blocks = (object_field, own_pair, near_block, near_pair, far_block, far_pair)
    keep_probe, send_probe, keep_grad, send_grad, weight = run_slots(
        place, offsets, counts, blocks, probe, patterns
    )

    got_probe = lax.ppermute(send_probe, "col", pair)
    got_grad = lax.ppermute(send_grad, "col", pair)
    mine = (keep_probe + got_probe).reshape(row_total, -1, width)
    mine = lax.all_to_all(mine, "row", 0, 0, tiled=True)
    mine = jnp.broadcast_to(jnp.sum(mine, axis=0, keepdims=True), mine.shape)
    strips = keep_grad + got_grad
    near_strip = lax.ppermute(strips[0], "row", near)
    far_strip = lax.ppermute(strips[1], "row", far)
    mine = lax.all_to_all(mine, "row", 0, 0, tiled=True).reshape(half, 2, width, width)
    other = lax.ppermute(mine, "col", pair)
    summed = jnp.where(
        core == 0,
        jnp.concatenate([mine, other], axis=0),
        jnp.concatenate([other, mine], axis=0),
    )
    object_grad = strips[2] + near_strip + far_strip
    object_field = object_field - object_rate * object_grad / weight[0, 0]
    probe = probe - probe_rate * summed / tile_total
    return (object_field, probe)


def solution(mesh):
    placed = (
        P(None, ("tilt", "row"), "col"),
        P("tilt", None, None, None),
        P(("tilt", "row"), "col", None, None, None),
        P(("tilt", "row"), "col", None, None),
        P(("tilt", "row"), "col"),
    )
    return jax.shard_map(
        body,
        mesh=mesh,
        in_specs=placed,
        out_specs=(P(None, ("tilt", "row"), "col"), P("tilt", None, None, None)),
        check_vma=False,
    )
```

```python
import jax
import jax.numpy as jnp
import numpy as np
from jax import lax
from jax.experimental import pallas as pl
from jax.experimental.pallas import tpu as pltpu
from jax.sharding import PartitionSpec as P


object_rate = 1.0
probe_rate = 1.0
epsilon = 1e-06


def split(value):
    high = value.astype(jnp.bfloat16)
    low = (value - high.astype(jnp.float32)).astype(jnp.bfloat16)
    return high, low


def host_tables(length):
    counter = np.arange(length)
    angle = -2.0 * np.pi / length * (counter[:, None] * counter[None, :] % length)
    cosine = (np.cos(angle) / np.sqrt(length)).astype(np.float32)
    sine = (np.sin(angle) / np.sqrt(length)).astype(np.float32)
    plain = np.block([[cosine, sine], [-sine, cosine]])
    conj = np.block([[cosine, -sine], [sine, cosine]])
    both = np.stack([plain, conj])
    high = both.astype(jnp.bfloat16)
    low = (both - high.astype(np.float32)).astype(jnp.bfloat16)
    return np.concatenate([high, low])


def stage_kernel(count, *refs):
    sources, targets, power_of = refs[:count], refs[count : 2 * count], refs[count]
    weight_ref, sems = refs[2 * count :]
    copies = [
        pltpu.make_async_copy(source, target, sems.at[index])
        for index, (source, target) in enumerate(zip(sources, targets))
    ]
    for copy in copies:
        copy.start()
    for copy in copies:
        copy.wait()
    power = jnp.zeros(power_of.shape[2:], jnp.float32)
    for k in range(power_of.shape[0]):
        power = power + power_of[k, 0] * power_of[k, 0] + power_of[k, 1] * power_of[k, 1]
    weight_ref[...] = jnp.full(weight_ref.shape, jnp.max(power) + epsilon, jnp.float32)


def stage(probe, *others):
    arrays = tuple(
        pltpu.with_memory_space_constraint(a, pltpu.HBM) for a in (probe,) + others
    )
    count = len(arrays)
    return pl.pallas_call(
        lambda *refs: stage_kernel(count, *refs),
        out_shape=tuple(jax.ShapeDtypeStruct(a.shape, a.dtype) for a in arrays)
        + (jax.ShapeDtypeStruct((8, probe.shape[-1]), jnp.float32),),
        in_specs=[pl.BlockSpec(memory_space=pltpu.HBM)] * count,
        out_specs=(pl.BlockSpec(memory_space=pltpu.VMEM),) * (count + 1),
        scratch_shapes=[pltpu.SemaphoreType.DMA((count,))],
        cost_estimate=pl.CostEstimate(
            flops=8 * probe.size,
            bytes_accessed=sum(2 * a.size * a.dtype.itemsize for a in arrays),
            transcendentals=0,
        ),
        compiler_params=pltpu.CompilerParams(vmem_limit_bytes=8 << 20),
        name="stage",
    )(*arrays)


def slots_kernel(
    offsets_hbm,
    counts_ref,
    own_ref,
    own_pair_ref,
    near_ref,
    near_pair_ref,
    far_ref,
    far_pair_ref,
    probe_ref,
    patterns_ref,
    tables_ref,
    keep_probe_ref,
    send_probe_ref,
    keep_grad_ref,
    send_grad_ref,
    offsets_ref,
    offsets_sem,
    frame,
    grad,
    term,
):
    fetch = pltpu.make_async_copy(offsets_hbm, offsets_ref, offsets_sem)
    fetch.start()
    modes = probe_ref.shape[0]
    width = probe_ref.shape[-1]
    slots = patterns_ref.shape[2]
    half = modes // 2
    core = lax.axis_index("col")
    odd = lax.rem(lax.axis_index("row"), 2)
    near_at = pl.multiple_of((1 - odd) * (2 * width), width)
    far_at = pl.multiple_of(odd * (2 * width), width)
    pair_at = 2 - 2 * core
    void_at = 2 * core

    empty = jnp.zeros((2, 3 * width, width), jnp.float32)
    frame[3] = empty
    frame[void_at] = empty
    frame[1, :, pl.ds(width, width), :] = own_ref[...]
    frame[1, :, pl.ds(near_at, width), :] = near_ref[...]
    frame[1, :, pl.ds(far_at, width), :] = far_ref[...]
    frame[pair_at, :, pl.ds(width, width), :] = own_pair_ref[...]
    frame[pair_at, :, pl.ds(near_at, width), :] = near_pair_ref[...]
    frame[pair_at, :, pl.ds(far_at, width), :] = far_pair_ref[...]
    grad[...] = jnp.zeros_like(grad)

    fetch.wait()

    lane = lax.broadcasted_iota(jnp.int32, (width, width), 1)

    def right(parts, which):
        value = jnp.concatenate([jnp.concatenate(part, axis=1) for part in parts], axis=0)
        high, low = split(value)
        table = jnp.concatenate(
            [tables_ref[which], tables_ref[which], tables_ref[2 + which]], axis=0
        )
        out = jnp.dot(
            jnp.concatenate([high, low, high], axis=1), table, preferred_element_type=jnp.float32
        )
        return [
            (out[k * width : (k + 1) * width, :width], out[k * width : (k + 1) * width, width:])
            for k in range(modes)
        ]

    def left(parts, which):
        value = jnp.concatenate([jnp.concatenate(part, axis=0) for part in parts], axis=1)
        high, low = split(value)
        table = jnp.concatenate(
            [tables_ref[1 - which], tables_ref[3 - which], tables_ref[1 - which]], axis=1
        )
        out = jnp.dot(
            table, jnp.concatenate([high, high, low], axis=0), preferred_element_type=jnp.float32
        )
        return [
            (out[:width, k * width : (k + 1) * width], out[width:, k * width : (k + 1) * width])
            for k in range(modes)
        ]

    for slot in range(slots):
        corner_y = offsets_ref[0, 0, slot, 0]
        corner_x = offsets_ref[0, 0, slot, 1]
        column = corner_x // width
        shift = corner_x - column * width
        back_shift = lax.rem(width - shift, width)
        rows = pl.ds(corner_y, width)
        live = (slot < counts_ref[0, 0]).astype(jnp.float32)

        window = []
        for part in range(2):
            both = jnp.where(
                lane >= shift, frame[column, part, rows, :], frame[column + 1, part, rows, :]
            )
            window.append(pltpu.roll(both, back_shift, 1))
        win_re, win_im = window

        exits = []
        for k in range(modes):
            probe_re, probe_im = probe_ref[k, 0], probe_ref[k, 1]
            exits.append(
                (
                    probe_re * win_re - probe_im * win_im,
                    probe_re * win_im + probe_im * win_re,
                )
            )
        far = left(right(exits, 0), 0)
        intensity = sum(re * re + im * im for re, im in far)
        misfit = (intensity - patterns_ref[0, 0, slot]) * live
        back = right(left([(misfit * re, misfit * im) for re, im in far], 1), 1)

        grad_re = jnp.zeros((width, width), jnp.float32)
        grad_im = jnp.zeros((width, width), jnp.float32)
        for k in range(modes):
            probe_re, probe_im = probe_ref[k, 0], probe_ref[k, 1]
            back_re, back_im = back[k]
            grad_re = grad_re + probe_re * back_re + probe_im * back_im
            grad_im = grad_im + probe_re * back_im - probe_im * back_re
            term_re = win_re * back_re + win_im * back_im
            term_im = win_re * back_im - win_im * back_re
            if slot == 0:
                term[k, 0] = term_re
                term[k, 1] = term_im
            else:
                term[k, 0] += term_re
                term[k, 1] += term_im
        for part, value in enumerate((grad_re, grad_im)):
            turned = pltpu.roll(value, shift, 1)
            grad[column, part, rows, :] += jnp.where(lane >= shift, turned, 0.0)
            grad[column + 1, part, rows, :] += jnp.where(lane >= shift, 0.0, turned)

    mine = core * half
    theirs = half - mine
    keep_probe_ref[...] = term[pl.ds(mine, half)]
    send_probe_ref[...] = term[pl.ds(theirs, half)]
    for index, place in enumerate((near_at, far_at, width)):
        keep_grad_ref[index] = grad[1, :, pl.ds(place, width), :]
        send_grad_ref[index] = grad[pair_at, :, pl.ds(place, width), :]


def run_slots(offsets, counts, blocks, probe, patterns, tables):
    modes, _, width, _ = probe.shape
    half = modes // 2
    smem = pl.BlockSpec(memory_space=pltpu.SMEM)
    vmem = pl.BlockSpec(memory_space=pltpu.VMEM)
    probe_half = jax.ShapeDtypeStruct((half, 2, width, width), jnp.float32)
    grad_rows = jax.ShapeDtypeStruct((3, 2, width, width), jnp.float32)
    slots = patterns.shape[2]
    return pl.pallas_call(
        slots_kernel,
        out_shape=(
            probe_half,
            probe_half,
            grad_rows,
            grad_rows,
        ),
        in_specs=[pl.BlockSpec(memory_space=pltpu.HBM), smem] + [vmem] * 9,
        out_specs=(vmem,) * 4,
        scratch_shapes=[
            pltpu.SMEM(offsets.shape, offsets.dtype),
            pltpu.SemaphoreType.DMA,
            pltpu.VMEM((4, 2, 3 * width, width), jnp.float32),
            pltpu.VMEM((4, 2, 3 * width, width), jnp.float32),
            pltpu.VMEM((modes, 2, width, width), jnp.float32),
        ],
        cost_estimate=pl.CostEstimate(
            flops=slots * modes * 4 * 3 * 8 * width**3,
            bytes_accessed=40 * width * width * 4,
            transcendentals=0,
        ),
        compiler_params=pltpu.CompilerParams(vmem_limit_bytes=16 << 20),
        name="slots",
    )(offsets, counts, *blocks, probe, patterns, tables)


def body(object_field, probe, patterns, offsets, counts):
    row_total = lax.axis_size("row")
    tile_total = row_total * lax.axis_size("col")
    modes, _, width, _ = probe.shape
    half = modes // 2
    core = lax.axis_index("col")

    pair = [(0, 1), (1, 0)]
    near = [(i, i ^ 1) for i in range(row_total)]
    far = [(i, i + 1) for i in range(1, row_total - 1, 2)]
    far = far + [(target, source) for source, target in far]

    near_block = lax.ppermute(object_field, "row", near)
    far_block = lax.ppermute(object_field, "row", far)
    own_pair = lax.ppermute(object_field, "col", pair)
    near_pair = lax.ppermute(near_block, "col", pair)
    far_pair = lax.ppermute(far_block, "col", pair)
    probe_here, patterns_here, own, tables, weight = stage(
        probe, patterns, object_field, jnp.asarray(host_tables(width))
    )
    blocks = (own, own_pair, near_block, near_pair, far_block, far_pair)
    keep_probe, send_probe, keep_grad, send_grad = run_slots(
        pltpu.with_memory_space_constraint(offsets, pltpu.HBM),
        counts,
        blocks,
        probe_here,
        patterns_here,
        tables,
    )

    got_probe = lax.ppermute(send_probe, "col", pair)
    got_grad = lax.ppermute(send_grad, "col", pair)
    mine = (keep_probe + got_probe).reshape(row_total, -1, width)
    mine = lax.all_to_all(mine, "row", 0, 0, tiled=True)
    mine = jnp.broadcast_to(jnp.sum(mine, axis=0, keepdims=True), mine.shape)
    strips = keep_grad + got_grad
    near_strip = lax.ppermute(strips[0], "row", near)
    far_strip = lax.ppermute(strips[1], "row", far)
    mine = lax.all_to_all(mine, "row", 0, 0, tiled=True).reshape(half, 2, width, width)
    other = lax.ppermute(mine, "col", pair)
    summed = jnp.where(
        core == 0,
        jnp.concatenate([mine, other], axis=0),
        jnp.concatenate([other, mine], axis=0),
    )
    object_grad = strips[2] + near_strip + far_strip
    grouped = object_grad.reshape(2, -1, *weight.shape)
    object_field = own - object_rate * (grouped / weight).reshape(object_field.shape)
    probe = probe_here - probe_rate * summed / tile_total
    return (object_field, probe)


def solution(mesh):
    placed = (
        P(None, ("tilt", "row"), "col"),
        P("tilt", None, None, None),
        P(("tilt", "row"), "col", None, None, None),
        P(("tilt", "row"), "col", None, None),
        P(("tilt", "row"), "col"),
    )

    return jax.shard_map(
        body,
        mesh=mesh,
        in_specs=placed,
        out_specs=(P(None, ("tilt", "row"), "col"), P("tilt", None, None, None)),
        check_vma=False,
    )
```

```python
import jax
import jax.numpy as jnp
import numpy as np
from jax import lax
from jax.experimental import pallas as pl
from jax.experimental.pallas import tpu as pltpu
from jax.sharding import PartitionSpec as P


object_rate = 1.0
probe_rate = 1.0
epsilon = 1e-06


def split(value):
    high = value.astype(jnp.bfloat16)
    low = (value - high.astype(jnp.float32)).astype(jnp.bfloat16)
    return high, low


def host_tables(length):
    counter = np.arange(length)
    angle = -2.0 * np.pi / length * (counter[:, None] * counter[None, :] % length)
    cosine = (np.cos(angle) / np.sqrt(length)).astype(np.float32)
    sine = (np.sin(angle) / np.sqrt(length)).astype(np.float32)
    plain = np.block([[cosine, sine], [-sine, cosine]])
    conj = np.block([[cosine, -sine], [sine, cosine]])
    both = np.stack([plain, conj])
    high = both.astype(jnp.bfloat16)
    low = (both - high.astype(np.float32)).astype(jnp.bfloat16)
    return np.concatenate([high, low])


def stage_kernel(count, *refs):
    sources, targets, power_of = refs[:count], refs[count : 2 * count], refs[count]
    weight_ref, sems = refs[2 * count :]
    copies = [
        pltpu.make_async_copy(source, target, sems.at[index])
        for index, (source, target) in enumerate(zip(sources, targets))
    ]
    for copy in copies:
        copy.start()
    for copy in copies:
        copy.wait()
    power = jnp.zeros(power_of.shape[2:], jnp.float32)
    for k in range(power_of.shape[0]):
        power = power + power_of[k, 0] * power_of[k, 0] + power_of[k, 1] * power_of[k, 1]
    weight_ref[...] = jnp.full(weight_ref.shape, jnp.max(power) + epsilon, jnp.float32)


def stage(probe, *others):
    arrays = tuple(
        pltpu.with_memory_space_constraint(a, pltpu.HBM) for a in (probe,) + others
    )
    count = len(arrays)
    return pl.pallas_call(
        lambda *refs: stage_kernel(count, *refs),
        out_shape=tuple(jax.ShapeDtypeStruct(a.shape, a.dtype) for a in arrays)
        + (jax.ShapeDtypeStruct((8, probe.shape[-1]), jnp.float32),),
        in_specs=[pl.BlockSpec(memory_space=pltpu.HBM)] * count,
        out_specs=(pl.BlockSpec(memory_space=pltpu.VMEM),) * (count + 1),
        scratch_shapes=[pltpu.SemaphoreType.DMA((count,))],
        cost_estimate=pl.CostEstimate(
            flops=8 * probe.size,
            bytes_accessed=sum(2 * a.size * a.dtype.itemsize for a in arrays),
            transcendentals=0,
        ),
        compiler_params=pltpu.CompilerParams(vmem_limit_bytes=8 << 20),
        name="stage",
    )(*arrays)


def product(pieces, tables_ref, which, on_left):
    width = pieces[0][0].shape[0]
    inner, outer = (0, 1) if on_left else (1, 0)
    value = jnp.concatenate([jnp.concatenate(piece, axis=inner) for piece in pieces], axis=outer)
    high, low = split(value)
    if on_left:
        table = jnp.concatenate(
            [tables_ref[1 - which], tables_ref[3 - which], tables_ref[1 - which]], axis=1
        )
        out = jnp.dot(
            table, jnp.concatenate([high, high, low], axis=0), preferred_element_type=jnp.float32
        )
    else:
        table = jnp.concatenate(
            [tables_ref[which], tables_ref[which], tables_ref[2 + which]], axis=0
        )
        out = jnp.dot(
            jnp.concatenate([high, low, high], axis=1), table, preferred_element_type=jnp.float32
        )
    found = []
    for index in range(len(pieces)):
        part = lax.slice_in_dim(out, index * width, (index + 1) * width, axis=outer)
        found.append(
            (
                lax.slice_in_dim(part, 0, width, axis=inner),
                lax.slice_in_dim(part, width, 2 * width, axis=inner),
            )
        )
    return found


def columns_of(corner_x, width, core):
    column = corner_x // width
    shift = corner_x - column * width
    pair_column = 2 - 2 * core
    found = []
    for place in (column, column + 1):
        is_pair = (place == pair_column).astype(jnp.int32)
        valid = jnp.logical_or(place == 1, place == pair_column)
        found.append((is_pair, valid))
    lane = lax.broadcasted_iota(jnp.int32, (width, width), 1)
    in_left = lane >= shift
    return shift, in_left, found


def first_kernel(
    offsets_hbm,
    counts_ref,
    own_ref,
    own_pair_ref,
    near_ref,
    near_pair_ref,
    far_ref,
    far_pair_ref,
    probe_ref,
    patterns_ref,
    tables_ref,
    send_probe_ref,
    window_ref,
    kept_ref,
    grad_ref,
    offsets_ref,
    offsets_sem,
    frame,
):
    fetch = pltpu.make_async_copy(offsets_hbm, offsets_ref, offsets_sem)
    fetch.start()
    modes = probe_ref.shape[0]
    width = probe_ref.shape[-1]
    slots = patterns_ref.shape[2]
    half = modes // 2
    core = lax.axis_index("col")
    odd = lax.rem(lax.axis_index("row"), 2)
    near_at = pl.multiple_of((1 - odd) * (2 * width), width)
    far_at = pl.multiple_of(odd * (2 * width), width)
    for index, (own, near, far) in enumerate(
        ((own_ref, near_ref, far_ref), (own_pair_ref, near_pair_ref, far_pair_ref))
    ):
        frame[index, :, pl.ds(width, width), :] = own[...]
        frame[index, :, pl.ds(near_at, width), :] = near[...]
        frame[index, :, pl.ds(far_at, width), :] = far[...]
    fetch.wait()

    mine = core * half
    order = [half - mine + k for k in range(half)] + [mine + k for k in range(half)]
    windows = []
    for slot in range(slots):
        rows = pl.ds(offsets_ref[0, 0, slot, 0], width)
        shift, in_left, blocks = columns_of(offsets_ref[0, 0, slot, 1], width, core)
        back_shift = lax.rem(width - shift, width)
        (left, left_valid), (right, right_valid) = blocks
        valid = jnp.logical_or(
            jnp.logical_and(in_left, left_valid),
            jnp.logical_and(jnp.logical_not(in_left), right_valid),
        )
        window = []
        for part in range(2):
            both = jnp.where(in_left, frame[left, part, rows, :], frame[right, part, rows, :])
            value = pltpu.roll(jnp.where(valid, both, 0.0), back_shift, 1)
            window_ref[slot, part] = value
            window.append(value)
        windows.append(window)

    values = []
    for win_re, win_im in windows:
        exits = []
        for k in order:
            probe_re, probe_im = probe_ref[k, 0], probe_ref[k, 1]
            exits.append(
                (
                    probe_re * win_re - probe_im * win_im,
                    probe_re * win_im + probe_im * win_re,
                )
            )
        values.append(exits)
    values = [product(value, tables_ref, 0, False) for value in values]
    values = [product(value, tables_ref, 0, True) for value in values]
    backs = []
    for slot, far in enumerate(values):
        live = (slot < counts_ref[0, 0]).astype(jnp.float32)
        intensity = sum(re * re + im * im for re, im in far)
        misfit = (intensity - patterns_ref[0, 0, slot]) * live
        for k in range(half):
            for part in range(2):
                kept_ref[slot, k, part] = misfit * far[half + k][part]
        backs.append([(misfit * re, misfit * im) for re, im in far[:half]])
    backs = [product(back, tables_ref, 1, True) for back in backs]
    backs = [product(back, tables_ref, 1, False) for back in backs]
    grads = combine(backs, probe_ref, order[:half], windows, send_probe_ref)
    for slot in range(slots):
        for part in range(2):
            grad_ref[slot, part] = grads[slot][part]


def combine(backs, probe_ref, order, windows, term_ref):
    grads = [[jnp.zeros_like(part) for part in window] for window in windows]
    for index, k in enumerate(order):
        probe_re, probe_im = probe_ref[k, 0], probe_ref[k, 1]
        term_re, term_im = 0.0, 0.0
        for slot, (win_re, win_im) in enumerate(windows):
            back_re, back_im = backs[slot][index]
            grads[slot][0] += probe_re * back_re + probe_im * back_im
            grads[slot][1] += probe_re * back_im - probe_im * back_re
            term_re += win_re * back_re + win_im * back_im
            term_im += win_re * back_im - win_im * back_re
        term_ref[index, 0] = term_re
        term_ref[index, 1] = term_im
    return grads


def second_kernel(
    offsets_hbm,
    probe_ref,
    tables_ref,
    window_ref,
    kept_ref,
    part_ref,
    keep_probe_ref,
    grad_ref,
    offsets_ref,
    offsets_sem,
):
    fetch = pltpu.make_async_copy(offsets_hbm, offsets_ref, offsets_sem)
    fetch.start()
    modes = probe_ref.shape[0]
    width = probe_ref.shape[-1]
    slots = window_ref.shape[0]
    half = modes // 2
    core = lax.axis_index("col")
    order = [core * half + k for k in range(half)]
    grad_ref[...] = jnp.zeros_like(grad_ref)
    backs = [
        [(kept_ref[slot, k, 0], kept_ref[slot, k, 1]) for k in range(half)]
        for slot in range(slots)
    ]
    windows = [[window_ref[slot, 0], window_ref[slot, 1]] for slot in range(slots)]
    backs = [product(back, tables_ref, 1, True) for back in backs]
    backs = [product(back, tables_ref, 1, False) for back in backs]
    grads = combine(backs, probe_ref, order, windows, keep_probe_ref)
    fetch.wait()
    for slot in range(slots):
        rows = pl.ds(offsets_ref[0, 0, slot, 0], width)
        shift, in_left, blocks = columns_of(offsets_ref[0, 0, slot, 1], width, core)
        (left, left_valid), (right, right_valid) = blocks
        to_left = jnp.logical_and(in_left, left_valid)
        to_right = jnp.logical_and(jnp.logical_not(in_left), right_valid)
        for part in range(2):
            turned = pltpu.roll(grads[slot][part] + part_ref[slot, part], shift, 1)
            grad_ref[left, part, rows, :] += jnp.where(to_left, turned, 0.0)
            grad_ref[right, part, rows, :] += jnp.where(to_right, turned, 0.0)


def run_first(offsets, counts, blocks, probe, patterns, tables):
    modes, _, width, _ = probe.shape
    half = modes // 2
    slots = patterns.shape[2]
    vmem = pl.BlockSpec(memory_space=pltpu.VMEM)
    images = lambda *lead: jax.ShapeDtypeStruct((*lead, 2, width, width), jnp.float32)
    return pl.pallas_call(
        first_kernel,
        out_shape=(images(half), images(slots), images(slots, half), images(slots)),
        in_specs=[
            pl.BlockSpec(memory_space=pltpu.HBM),
            pl.BlockSpec(memory_space=pltpu.SMEM),
        ]
        + [vmem] * 9,
        out_specs=(vmem,) * 4,
        scratch_shapes=[
            pltpu.SMEM(offsets.shape, offsets.dtype),
            pltpu.SemaphoreType.DMA,
            pltpu.VMEM((2, 2, 3 * width, width), jnp.float32),
        ],
        cost_estimate=pl.CostEstimate(
            flops=slots * modes * 3 * 3 * 8 * width**3,
            bytes_accessed=40 * width * width * 4,
            transcendentals=0,
        ),
        compiler_params=pltpu.CompilerParams(vmem_limit_bytes=16 << 20),
        name="first",
    )(offsets, counts, *blocks, probe, patterns, tables)


def run_second(offsets, probe, tables, window, kept, part):
    modes, _, width, _ = probe.shape
    half = modes // 2
    slots = window.shape[0]
    vmem = pl.BlockSpec(memory_space=pltpu.VMEM)
    return pl.pallas_call(
        second_kernel,
        out_shape=(
            jax.ShapeDtypeStruct((half, 2, width, width), jnp.float32),
            jax.ShapeDtypeStruct((2, 2, 3 * width, width), jnp.float32),
        ),
        in_specs=[pl.BlockSpec(memory_space=pltpu.HBM)] + [vmem] * 5,
        out_specs=(vmem,) * 2,
        scratch_shapes=[
            pltpu.SMEM(offsets.shape, offsets.dtype),
            pltpu.SemaphoreType.DMA,
        ],
        cost_estimate=pl.CostEstimate(
            flops=slots * modes * 3 * 8 * width**3,
            bytes_accessed=30 * width * width * 4,
            transcendentals=0,
        ),
        compiler_params=pltpu.CompilerParams(vmem_limit_bytes=16 << 20),
        name="second",
    )(offsets, probe, tables, window, kept, part)


def member_order(count):
    pairs = count // 2
    middle = (pairs - 1) // 2
    order = []
    for step in range(pairs):
        near = (step + 1) // 2
        at = middle + near if step % 2 else middle - near
        order.extend((2 * at + 1, 2 * at))
    return order


def body(object_field, probe, patterns, offsets, counts):
    row_total = lax.axis_size("row")
    tile_total = row_total * lax.axis_size("col")
    modes, _, width, _ = probe.shape
    half = modes // 2
    core = lax.axis_index("col")

    pair = [(0, 1), (1, 0)]
    near = [(i, i ^ 1) for i in range(row_total)]
    far = [(i, i + 1) for i in range(1, row_total - 1, 2)]
    far = far + [(target, source) for source, target in far]

    near_block = lax.ppermute(object_field, "row", near)
    far_block = lax.ppermute(object_field, "row", far)
    own_pair = lax.ppermute(object_field, "col", pair)
    near_pair = lax.ppermute(near_block, "col", pair)
    far_pair = lax.ppermute(far_block, "col", pair)
    probe_here, patterns_here, own, tables, weight = stage(
        probe, patterns, object_field, jnp.asarray(host_tables(width))
    )
    blocks = (own, own_pair, near_block, near_pair, far_block, far_pair)
    offsets = pltpu.with_memory_space_constraint(offsets, pltpu.HBM)
    send_probe, window, kept, part = run_first(
        offsets, counts, blocks, probe_here, patterns_here, tables
    )
    got_probe = lax.ppermute(send_probe, "col", pair)
    keep_probe, grads = run_second(offsets, probe_here, tables, window, kept, part)
    got_grad = lax.ppermute(grads[1], "col", pair)

    members = [member_order(row_total)]
    mine = (keep_probe + got_probe).reshape(row_total, -1, width)
    mine = lax.all_to_all(mine, "row", 0, 0, tiled=True, axis_index_groups=members)
    mine = jnp.broadcast_to(jnp.sum(mine, axis=0, keepdims=True), mine.shape)
    strips = grads[0] + got_grad
    odd = lax.axis_index("row") % 2
    near_strip = lax.dynamic_slice_in_dim(strips, (1 - odd) * (2 * width), width, axis=1)
    far_strip = lax.dynamic_slice_in_dim(strips, odd * (2 * width), width, axis=1)
    near_strip = lax.ppermute(near_strip, "row", near)
    far_strip = lax.ppermute(far_strip, "row", far)
    mine = lax.all_to_all(mine, "row", 0, 0, tiled=True, axis_index_groups=members)
    mine = mine.reshape(half, 2, width, width)
    other = lax.ppermute(mine, "col", pair)
    summed = jnp.where(
        core == 0,
        jnp.concatenate([mine, other], axis=0),
        jnp.concatenate([other, mine], axis=0),
    )
    object_grad = strips[:, width : 2 * width] + near_strip + far_strip
    grouped = object_grad.reshape(2, -1, *weight.shape)
    object_field = own - object_rate * (grouped / weight).reshape(object_field.shape)
    probe = probe_here - probe_rate * summed / tile_total
    return (object_field, probe)


def solution(mesh):
    placed = (
        P(None, ("tilt", "row"), "col"),
        P("tilt", None, None, None),
        P(("tilt", "row"), "col", None, None, None),
        P(("tilt", "row"), "col", None, None),
        P(("tilt", "row"), "col"),
    )

    return jax.shard_map(
        body,
        mesh=mesh,
        in_specs=placed,
        out_specs=(P(None, ("tilt", "row"), "col"), P("tilt", None, None, None)),
        check_vma=False,
    )
```

```python
import functools

import jax
import jax.numpy as jnp
import numpy as np
from jax import lax
from jax.experimental import pallas as pl
from jax.experimental.pallas import tpu as pltpu
from jax.sharding import PartitionSpec as P


object_rate = 1.0
probe_rate = 1.0
epsilon = 1e-06


def split(value):
    high = value.astype(jnp.bfloat16)
    low = (value - high.astype(jnp.float32)).astype(jnp.bfloat16)
    return high, low


def host_tables(length):
    counter = np.arange(length)
    angle = -2.0 * np.pi / length * (counter[:, None] * counter[None, :] % length)
    cosine = (np.cos(angle) / np.sqrt(length)).astype(np.float32)
    sine = (np.sin(angle) / np.sqrt(length)).astype(np.float32)
    plain = np.block([[cosine, sine], [-sine, cosine]])
    conj = np.block([[cosine, -sine], [sine, cosine]])
    both = np.stack([plain, conj])
    high = both.astype(jnp.bfloat16)
    low = (both - high.astype(np.float32)).astype(jnp.bfloat16)
    return np.concatenate([high, low])


def stage_kernel(count, *refs):
    sources, targets, power_of = refs[:count], refs[count : 2 * count], refs[count]
    weight_ref, sems = refs[2 * count :]
    copies = [
        pltpu.make_async_copy(source, target, sems.at[index])
        for index, (source, target) in enumerate(zip(sources, targets))
    ]
    for copy in copies:
        copy.start()
    for copy in copies:
        copy.wait()
    power = jnp.zeros(power_of.shape[2:], jnp.float32)
    for k in range(power_of.shape[0]):
        power = power + power_of[k, 0] * power_of[k, 0] + power_of[k, 1] * power_of[k, 1]
    weight_ref[...] = jnp.full(weight_ref.shape, jnp.max(power) + epsilon, jnp.float32)


def stage(probe, *others):
    arrays = tuple(
        pltpu.with_memory_space_constraint(a, pltpu.HBM) for a in (probe,) + others
    )
    count = len(arrays)
    return pl.pallas_call(
        lambda *refs: stage_kernel(count, *refs),
        out_shape=tuple(jax.ShapeDtypeStruct(a.shape, a.dtype) for a in arrays)
        + (jax.ShapeDtypeStruct((8, probe.shape[-1]), jnp.float32),),
        in_specs=[pl.BlockSpec(memory_space=pltpu.HBM)] * count,
        out_specs=(pl.BlockSpec(memory_space=pltpu.VMEM),) * (count + 1),
        scratch_shapes=[pltpu.SemaphoreType.DMA((count,))],
        cost_estimate=pl.CostEstimate(
            flops=8 * probe.size,
            bytes_accessed=sum(2 * a.size * a.dtype.itemsize for a in arrays),
            transcendentals=0,
        ),
        compiler_params=pltpu.CompilerParams(vmem_limit_bytes=8 << 20),
        name="stage",
    )(*arrays)


def product(pieces, tables_ref, which, on_left):
    width = pieces[0][0].shape[0]
    inner, outer = (0, 1) if on_left else (1, 0)
    value = jnp.concatenate([jnp.concatenate(piece, axis=inner) for piece in pieces], axis=outer)
    high, low = split(value)
    if on_left:
        table = jnp.concatenate(
            [tables_ref[1 - which], tables_ref[3 - which], tables_ref[1 - which]], axis=1
        )
        out = jnp.dot(
            table, jnp.concatenate([high, high, low], axis=0), preferred_element_type=jnp.float32
        )
    else:
        table = jnp.concatenate(
            [tables_ref[which], tables_ref[which], tables_ref[2 + which]], axis=0
        )
        out = jnp.dot(
            jnp.concatenate([high, low, high], axis=1), table, preferred_element_type=jnp.float32
        )
    found = []
    for index in range(len(pieces)):
        part = lax.slice_in_dim(out, index * width, (index + 1) * width, axis=outer)
        found.append(
            (
                lax.slice_in_dim(part, 0, width, axis=inner),
                lax.slice_in_dim(part, width, 2 * width, axis=inner),
            )
        )
    return found


def columns_of(corner_x, width, core):
    column = corner_x // width
    shift = corner_x - column * width
    pair_column = 2 - 2 * core
    found = []
    for place in (column, column + 1):
        is_pair = (place == pair_column).astype(jnp.int32)
        valid = jnp.logical_or(place == 1, place == pair_column)
        found.append((is_pair, valid))
    lane = lax.broadcasted_iota(jnp.int32, (width, width), 1)
    in_left = lane >= shift
    return shift, in_left, found


def first_kernel(
    offsets_hbm,
    counts_ref,
    own_ref,
    own_pair_ref,
    near_ref,
    near_pair_ref,
    far_ref,
    far_pair_ref,
    probe_ref,
    patterns_ref,
    tables_ref,
    send_probe_ref,
    window_ref,
    kept_ref,
    grad_ref,
    offsets_ref,
    offsets_sem,
    frame,
):
    fetch = pltpu.make_async_copy(offsets_hbm, offsets_ref, offsets_sem)
    fetch.start()
    modes = probe_ref.shape[0]
    width = probe_ref.shape[-1]
    slots = patterns_ref.shape[2]
    half = modes // 2
    core = lax.axis_index("col")
    odd = lax.rem(lax.axis_index("row"), 2)
    near_at = pl.multiple_of((1 - odd) * (2 * width), width)
    far_at = pl.multiple_of(odd * (2 * width), width)
    for index, (own, near, far) in enumerate(
        ((own_ref, near_ref, far_ref), (own_pair_ref, near_pair_ref, far_pair_ref))
    ):
        frame[index, :, pl.ds(width, width), :] = own[...]
        frame[index, :, pl.ds(near_at, width), :] = near[...]
        frame[index, :, pl.ds(far_at, width), :] = far[...]
    fetch.wait()

    mine = core * half
    order = [half - mine + k for k in range(half)] + [mine + k for k in range(half)]
    windows = []
    for slot in range(slots):
        rows = pl.ds(offsets_ref[0, 0, slot, 0], width)
        shift, in_left, blocks = columns_of(offsets_ref[0, 0, slot, 1], width, core)
        back_shift = lax.rem(width - shift, width)
        (left, left_valid), (right, right_valid) = blocks
        valid = jnp.logical_or(
            jnp.logical_and(in_left, left_valid),
            jnp.logical_and(jnp.logical_not(in_left), right_valid),
        )
        window = []
        for part in range(2):
            both = jnp.where(in_left, frame[left, part, rows, :], frame[right, part, rows, :])
            value = pltpu.roll(jnp.where(valid, both, 0.0), back_shift, 1)
            window_ref[slot, part] = value
            window.append(value)
        windows.append(window)

    values = []
    for win_re, win_im in windows:
        exits = []
        for k in order:
            probe_re, probe_im = probe_ref[k, 0], probe_ref[k, 1]
            exits.append(
                (
                    probe_re * win_re - probe_im * win_im,
                    probe_re * win_im + probe_im * win_re,
                )
            )
        values.append(exits)
    values = [product(value, tables_ref, 0, False) for value in values]
    values = [product(value, tables_ref, 0, True) for value in values]
    backs = []
    for slot, far in enumerate(values):
        live = (slot < counts_ref[0, 0]).astype(jnp.float32)
        intensity = sum(re * re + im * im for re, im in far)
        misfit = (intensity - patterns_ref[0, 0, slot]) * live
        for k in range(half):
            for part in range(2):
                kept_ref[slot, k, part] = misfit * far[half + k][part]
        backs.append([(misfit * re, misfit * im) for re, im in far[:half]])
    backs = [product(back, tables_ref, 1, True) for back in backs]
    backs = [product(back, tables_ref, 1, False) for back in backs]
    grads = combine(backs, probe_ref, order[:half], windows, send_probe_ref)
    for slot in range(slots):
        for part in range(2):
            grad_ref[slot, part] = grads[slot][part]


def combine(backs, probe_ref, order, windows, term_ref):
    grads = [[jnp.zeros_like(part) for part in window] for window in windows]
    for index, k in enumerate(order):
        probe_re, probe_im = probe_ref[k, 0], probe_ref[k, 1]
        term_re, term_im = 0.0, 0.0
        for slot, (win_re, win_im) in enumerate(windows):
            back_re, back_im = backs[slot][index]
            grads[slot][0] += probe_re * back_re + probe_im * back_im
            grads[slot][1] += probe_re * back_im - probe_im * back_re
            term_re += win_re * back_re + win_im * back_im
            term_im += win_re * back_im - win_im * back_re
        term_ref[index, 0] = term_re
        term_ref[index, 1] = term_im
    return grads


def second_kernel(
    offsets_hbm,
    probe_ref,
    tables_ref,
    window_ref,
    kept_ref,
    part_ref,
    keep_probe_ref,
    grad_ref,
    offsets_ref,
    offsets_sem,
):
    fetch = pltpu.make_async_copy(offsets_hbm, offsets_ref, offsets_sem)
    fetch.start()
    modes = probe_ref.shape[0]
    width = probe_ref.shape[-1]
    slots = window_ref.shape[0]
    half = modes // 2
    core = lax.axis_index("col")
    order = [core * half + k for k in range(half)]
    grad_ref[...] = jnp.zeros_like(grad_ref)
    backs = [
        [(kept_ref[slot, k, 0], kept_ref[slot, k, 1]) for k in range(half)]
        for slot in range(slots)
    ]
    windows = [[window_ref[slot, 0], window_ref[slot, 1]] for slot in range(slots)]
    backs = [product(back, tables_ref, 1, True) for back in backs]
    backs = [product(back, tables_ref, 1, False) for back in backs]
    grads = combine(backs, probe_ref, order, windows, keep_probe_ref)
    fetch.wait()
    for slot in range(slots):
        rows = pl.ds(offsets_ref[0, 0, slot, 0], width)
        shift, in_left, blocks = columns_of(offsets_ref[0, 0, slot, 1], width, core)
        (left, left_valid), (right, right_valid) = blocks
        to_left = jnp.logical_and(in_left, left_valid)
        to_right = jnp.logical_and(jnp.logical_not(in_left), right_valid)
        for part in range(2):
            turned = pltpu.roll(grads[slot][part] + part_ref[slot, part], shift, 1)
            grad_ref[left, part, rows, :] += jnp.where(to_left, turned, 0.0)
            grad_ref[right, part, rows, :] += jnp.where(to_right, turned, 0.0)


def run_first(offsets, counts, blocks, probe, patterns, tables):
    modes, _, width, _ = probe.shape
    half = modes // 2
    slots = patterns.shape[2]
    vmem = pl.BlockSpec(memory_space=pltpu.VMEM)
    images = lambda *lead: jax.ShapeDtypeStruct((*lead, 2, width, width), jnp.float32)
    return pl.pallas_call(
        first_kernel,
        out_shape=(images(half), images(slots), images(slots, half), images(slots)),
        in_specs=[
            pl.BlockSpec(memory_space=pltpu.HBM),
            pl.BlockSpec(memory_space=pltpu.SMEM),
        ]
        + [vmem] * 9,
        out_specs=(vmem,) * 4,
        scratch_shapes=[
            pltpu.SMEM(offsets.shape, offsets.dtype),
            pltpu.SemaphoreType.DMA,
            pltpu.VMEM((2, 2, 3 * width, width), jnp.float32),
        ],
        cost_estimate=pl.CostEstimate(
            flops=slots * modes * 3 * 3 * 8 * width**3,
            bytes_accessed=40 * width * width * 4,
            transcendentals=0,
        ),
        compiler_params=pltpu.CompilerParams(vmem_limit_bytes=16 << 20),
        name="first",
    )(offsets, counts, *blocks, probe, patterns, tables)


def run_second(offsets, probe, tables, window, kept, part):
    modes, _, width, _ = probe.shape
    half = modes // 2
    slots = window.shape[0]
    vmem = pl.BlockSpec(memory_space=pltpu.VMEM)
    return pl.pallas_call(
        second_kernel,
        out_shape=(
            jax.ShapeDtypeStruct((half, 2, width, width), jnp.float32),
            jax.ShapeDtypeStruct((2, 2, 3 * width, width), jnp.float32),
        ),
        in_specs=[pl.BlockSpec(memory_space=pltpu.HBM)] + [vmem] * 5,
        out_specs=(vmem,) * 2,
        scratch_shapes=[
            pltpu.SMEM(offsets.shape, offsets.dtype),
            pltpu.SemaphoreType.DMA,
        ],
        cost_estimate=pl.CostEstimate(
            flops=slots * modes * 3 * 8 * width**3,
            bytes_accessed=30 * width * width * 4,
            transcendentals=0,
        ),
        compiler_params=pltpu.CompilerParams(vmem_limit_bytes=16 << 20),
        name="second",
    )(offsets, probe, tables, window, kept, part)


def total_kernel(parts_ref, out_ref):
    total = parts_ref[0]
    for index in range(1, parts_ref.shape[0]):
        total = total + parts_ref[index]
    for index in range(parts_ref.shape[0]):
        out_ref[index] = total


def strips_kernel(grads_ref, got_ref, middle_ref, near_ref, far_ref):
    width = got_ref.shape[-1]
    odd = lax.rem(lax.axis_index("row"), 2)
    near_at = pl.multiple_of((1 - odd) * (2 * width), width)
    far_at = pl.multiple_of(odd * (2 * width), width)
    for out_ref, place in ((middle_ref, width), (near_ref, near_at), (far_ref, far_at)):
        rows = pl.ds(place, width)
        out_ref[...] = grads_ref[0, :, rows, :] + got_ref[:, rows, :]


def object_kernel(own_ref, middle_ref, near_ref, far_ref, weight_ref, out_ref):
    weight = weight_ref[...]
    grad = (middle_ref[...] + near_ref[...] + far_ref[...]).reshape(-1, *weight.shape)
    out = own_ref[...].reshape(grad.shape) - object_rate * (grad / weight)
    out_ref[...] = out.reshape(own_ref.shape)


def probe_kernel(tile_total, probe_ref, mine_ref, other_ref, out_ref):
    half = mine_ref.shape[0]
    core = lax.axis_index("col")
    for part_ref, which in ((mine_ref, core), (other_ref, 1 - core)):
        modes = pl.ds(which * half, half)
        out_ref[modes] = probe_ref[modes] - probe_rate * part_ref[...] / tile_total


def in_vmem(kernel, shapes, *operands):
    vmem = pl.BlockSpec(memory_space=pltpu.VMEM)
    out = tuple(jax.ShapeDtypeStruct(shape, jnp.float32) for shape in shapes)
    size = sum(a.size for a in out + operands)
    return pl.pallas_call(
        kernel,
        out_shape=out if len(out) > 1 else out[0],
        in_specs=[vmem] * len(operands),
        out_specs=(vmem,) * len(out) if len(out) > 1 else vmem,
        cost_estimate=pl.CostEstimate(flops=size, bytes_accessed=4 * size, transcendentals=0),
        compiler_params=pltpu.CompilerParams(vmem_limit_bytes=8 << 20),
    )(*operands)


def member_order(count):
    pairs = count // 2
    middle = (pairs - 1) // 2
    order = []
    for step in range(pairs):
        near = (step + 1) // 2
        at = middle + near if step % 2 else middle - near
        order.extend((2 * at + 1, 2 * at))
    return order


def body(object_field, probe, patterns, offsets, counts):
    row_total = lax.axis_size("row")
    tile_total = row_total * lax.axis_size("col")
    modes, _, width, _ = probe.shape
    half = modes // 2

    pair = [(0, 1), (1, 0)]
    near = [(i, i ^ 1) for i in range(row_total)]
    far = [(i, i + 1) for i in range(1, row_total - 1, 2)]
    far = far + [(target, source) for source, target in far]

    near_block = lax.ppermute(object_field, "row", near)
    far_block = lax.ppermute(object_field, "row", far)
    own_pair = lax.ppermute(object_field, "col", pair)
    near_pair = lax.ppermute(near_block, "col", pair)
    far_pair = lax.ppermute(far_block, "col", pair)
    probe_here, patterns_here, own, tables, weight = stage(
        probe, patterns, object_field, jnp.asarray(host_tables(width))
    )
    blocks = (own, own_pair, near_block, near_pair, far_block, far_pair)
    offsets = pltpu.with_memory_space_constraint(offsets, pltpu.HBM)
    send_probe, window, kept, part = run_first(
        offsets, counts, blocks, probe_here, patterns_here, tables
    )
    got_probe = lax.ppermute(send_probe, "col", pair)
    keep_probe, grads = run_second(offsets, probe_here, tables, window, kept, part)
    got_grad = lax.ppermute(grads[1], "col", pair)

    members = [member_order(row_total)]
    mine = (keep_probe + got_probe).reshape(row_total, -1, width)
    mine = lax.all_to_all(mine, "row", 0, 0, tiled=True, axis_index_groups=members)
    mine = in_vmem(total_kernel, [mine.shape], mine)
    block = own.shape
    middle, near_strip, far_strip = in_vmem(
        strips_kernel, [block, block, block], grads, got_grad
    )
    near_strip = lax.ppermute(near_strip, "row", near)
    far_strip = lax.ppermute(far_strip, "row", far)
    mine = lax.all_to_all(mine, "row", 0, 0, tiled=True, axis_index_groups=members)
    mine = mine.reshape(half, 2, width, width)
    other = lax.ppermute(mine, "col", pair)
    object_field = in_vmem(
        object_kernel, [block], own, middle, near_strip, far_strip, weight
    )
    probe = in_vmem(
        functools.partial(probe_kernel, tile_total), [probe.shape], probe_here, mine, other
    )
    return (object_field, probe)


def solution(mesh):
    placed = (
        P(None, ("tilt", "row"), "col"),
        P("tilt", None, None, None),
        P(("tilt", "row"), "col", None, None, None),
        P(("tilt", "row"), "col", None, None),
        P(("tilt", "row"), "col"),
    )

    return jax.shard_map(
        body,
        mesh=mesh,
        in_specs=placed,
        out_specs=(P(None, ("tilt", "row"), "col"), P("tilt", None, None, None)),
        check_vma=False,
    )
```

```python
import functools

import jax
import jax.numpy as jnp
import numpy as np
from jax import lax
from jax.experimental import pallas as pl
from jax.experimental.pallas import tpu as pltpu
from jax.sharding import PartitionSpec as P


object_rate = 1.0
probe_rate = 1.0
epsilon = 1e-06


def split(value):
    high = value.astype(jnp.bfloat16)
    low = (value - high.astype(jnp.float32)).astype(jnp.bfloat16)
    return high, low


def host_tables(length):
    counter = np.arange(length)
    angle = -2.0 * np.pi / length * (counter[:, None] * counter[None, :] % length)
    cosine = (np.cos(angle) / np.sqrt(length)).astype(np.float32)
    sine = (np.sin(angle) / np.sqrt(length)).astype(np.float32)
    plain = np.block([[cosine, sine], [-sine, cosine]])
    conj = np.block([[cosine, -sine], [sine, cosine]])
    both = np.stack([plain, conj])
    high = both.astype(jnp.bfloat16)
    low = (both - high.astype(np.float32)).astype(jnp.bfloat16)
    return np.concatenate([high, low])


def stage_kernel(count, *refs):
    sources, targets, power_of = refs[:count], refs[count : 2 * count], refs[count]
    weight_ref, sems = refs[2 * count :]
    copies = [
        pltpu.make_async_copy(source, target, sems.at[index])
        for index, (source, target) in enumerate(zip(sources, targets))
    ]
    for copy in copies:
        copy.start()
    for copy in copies:
        copy.wait()
    power = jnp.zeros(power_of.shape[2:], jnp.float32)
    for k in range(power_of.shape[0]):
        power = power + power_of[k, 0] * power_of[k, 0] + power_of[k, 1] * power_of[k, 1]
    weight_ref[...] = jnp.full(weight_ref.shape, jnp.max(power) + epsilon, jnp.float32)


def stage(probe, *others):
    arrays = tuple(
        pltpu.with_memory_space_constraint(a, pltpu.HBM) for a in (probe,) + others
    )
    count = len(arrays)
    return pl.pallas_call(
        lambda *refs: stage_kernel(count, *refs),
        out_shape=tuple(jax.ShapeDtypeStruct(a.shape, a.dtype) for a in arrays)
        + (jax.ShapeDtypeStruct((8, probe.shape[-1]), jnp.float32),),
        in_specs=[pl.BlockSpec(memory_space=pltpu.HBM)] * count,
        out_specs=(pl.BlockSpec(memory_space=pltpu.VMEM),) * (count + 1),
        scratch_shapes=[pltpu.SemaphoreType.DMA((count,))],
        cost_estimate=pl.CostEstimate(
            flops=8 * probe.size,
            bytes_accessed=sum(2 * a.size * a.dtype.itemsize for a in arrays),
            transcendentals=0,
        ),
        compiler_params=pltpu.CompilerParams(vmem_limit_bytes=8 << 20),
        name="stage",
    )(*arrays)


def product(pieces, tables_ref, which, on_left):
    width = pieces[0][0].shape[0]
    inner, outer = (0, 1) if on_left else (1, 0)
    value = jnp.concatenate([jnp.concatenate(piece, axis=inner) for piece in pieces], axis=outer)
    high, low = split(value)
    if on_left:
        table = jnp.concatenate(
            [tables_ref[1 - which], tables_ref[1 - which], tables_ref[3 - which]], axis=1
        )
        out = jnp.dot(
            table, jnp.concatenate([high, low, high], axis=0), preferred_element_type=jnp.float32
        )
    else:
        table = jnp.concatenate(
            [tables_ref[which], tables_ref[2 + which], tables_ref[which]], axis=0
        )
        out = jnp.dot(
            jnp.concatenate([high, high, low], axis=1), table, preferred_element_type=jnp.float32
        )
    found = []
    for index in range(len(pieces)):
        part = lax.slice_in_dim(out, index * width, (index + 1) * width, axis=outer)
        found.append(
            (
                lax.slice_in_dim(part, 0, width, axis=inner),
                lax.slice_in_dim(part, width, 2 * width, axis=inner),
            )
        )
    return found


def in_groups(value, size, *rest):
    found = []
    for at in range(0, len(value), size):
        found += product(value[at : at + size], *rest)
    return found


def columns_of(corner_x, width, core):
    column = corner_x // width
    shift = corner_x - column * width
    pair_column = 2 - 2 * core
    found = []
    for place in (column, column + 1):
        is_pair = (place == pair_column).astype(jnp.int32)
        valid = jnp.logical_or(place == 1, place == pair_column)
        found.append((is_pair, valid))
    lane = lax.broadcasted_iota(jnp.int32, (width, width), 1)
    in_left = lane >= shift
    return shift, in_left, found


def first_kernel(
    offsets_hbm,
    counts_ref,
    own_ref,
    own_pair_ref,
    near_ref,
    near_pair_ref,
    far_ref,
    far_pair_ref,
    probe_ref,
    patterns_ref,
    tables_ref,
    send_probe_ref,
    window_ref,
    kept_ref,
    grad_ref,
    offsets_ref,
    offsets_sem,
    frame,
):
    fetch = pltpu.make_async_copy(offsets_hbm, offsets_ref, offsets_sem)
    fetch.start()
    modes = probe_ref.shape[0]
    width = probe_ref.shape[-1]
    slots = patterns_ref.shape[2]
    half = modes // 2
    core = lax.axis_index("col")
    odd = lax.rem(lax.axis_index("row"), 2)
    near_at = pl.multiple_of((1 - odd) * (2 * width), width)
    far_at = pl.multiple_of(odd * (2 * width), width)
    for index, (own, near, far) in enumerate(
        ((own_ref, near_ref, far_ref), (own_pair_ref, near_pair_ref, far_pair_ref))
    ):
        frame[index, :, pl.ds(width, width), :] = own[...]
        frame[index, :, pl.ds(near_at, width), :] = near[...]
        frame[index, :, pl.ds(far_at, width), :] = far[...]
    fetch.wait()

    mine = core * half
    order = [half - mine + k for k in range(half)] + [mine + k for k in range(half)]
    windows = []
    for slot in range(slots):
        rows = pl.ds(offsets_ref[0, 0, slot, 0], width)
        shift, in_left, blocks = columns_of(offsets_ref[0, 0, slot, 1], width, core)
        back_shift = lax.rem(width - shift, width)
        (left, left_valid), (right, right_valid) = blocks
        valid = jnp.logical_or(
            jnp.logical_and(in_left, left_valid),
            jnp.logical_and(jnp.logical_not(in_left), right_valid),
        )
        window = []
        for part in range(2):
            both = jnp.where(in_left, frame[left, part, rows, :], frame[right, part, rows, :])
            value = pltpu.roll(jnp.where(valid, both, 0.0), back_shift, 1)
            window_ref[slot, part] = value
            window.append(value)
        windows.append(window)

    values = []
    for win_re, win_im in windows:
        exits = []
        for k in order:
            probe_re, probe_im = probe_ref[k, 0], probe_ref[k, 1]
            exits.append(
                (
                    probe_re * win_re - probe_im * win_im,
                    probe_re * win_im + probe_im * win_re,
                )
            )
        values.append(exits)
    values = [in_groups(value, 2, tables_ref, 0, False) for value in values]
    values = [in_groups(value, 4, tables_ref, 0, True) for value in values]
    backs = []
    for slot, far in enumerate(values):
        live = (slot < counts_ref[0, 0]).astype(jnp.float32)
        intensity = sum(re * re + im * im for re, im in far)
        misfit = (intensity - patterns_ref[0, 0, slot]) * live
        for k in range(half):
            for part in range(2):
                kept_ref[slot, k, part] = misfit * far[half + k][part]
        backs.append([(misfit * re, misfit * im) for re, im in far[:half]])
    backs = [in_groups(back, 2, tables_ref, 1, True) for back in backs]
    backs = [in_groups(back, 2, tables_ref, 1, False) for back in backs]
    grads = combine(backs, probe_ref, order[:half], windows, send_probe_ref)
    for slot in range(slots):
        for part in range(2):
            grad_ref[slot, part] = grads[slot][part]


def combine(backs, probe_ref, order, windows, term_ref):
    grads = [[jnp.zeros_like(part) for part in window] for window in windows]
    for index, k in enumerate(order):
        probe_re, probe_im = probe_ref[k, 0], probe_ref[k, 1]
        term_re, term_im = 0.0, 0.0
        for slot, (win_re, win_im) in enumerate(windows):
            back_re, back_im = backs[slot][index]
            grads[slot][0] += probe_re * back_re + probe_im * back_im
            grads[slot][1] += probe_re * back_im - probe_im * back_re
            term_re += win_re * back_re + win_im * back_im
            term_im += win_re * back_im - win_im * back_re
        term_ref[index, 0] = term_re
        term_ref[index, 1] = term_im
    return grads


def second_kernel(
    offsets_hbm,
    probe_ref,
    tables_ref,
    window_ref,
    kept_ref,
    part_ref,
    keep_probe_ref,
    grad_ref,
    offsets_ref,
    offsets_sem,
):
    fetch = pltpu.make_async_copy(offsets_hbm, offsets_ref, offsets_sem)
    fetch.start()
    modes = probe_ref.shape[0]
    width = probe_ref.shape[-1]
    slots = window_ref.shape[0]
    half = modes // 2
    core = lax.axis_index("col")
    order = [core * half + k for k in range(half)]
    grad_ref[...] = jnp.zeros_like(grad_ref)
    backs = [
        [(kept_ref[slot, k, 0], kept_ref[slot, k, 1]) for k in range(half)]
        for slot in range(slots)
    ]
    windows = [[window_ref[slot, 0], window_ref[slot, 1]] for slot in range(slots)]
    backs = [in_groups(back, 2, tables_ref, 1, True) for back in backs]
    backs = [in_groups(back, 2, tables_ref, 1, False) for back in backs]
    grads = combine(backs, probe_ref, order, windows, keep_probe_ref)
    fetch.wait()
    for slot in range(slots):
        rows = pl.ds(offsets_ref[0, 0, slot, 0], width)
        shift, in_left, blocks = columns_of(offsets_ref[0, 0, slot, 1], width, core)
        (left, left_valid), (right, right_valid) = blocks
        to_left = jnp.logical_and(in_left, left_valid)
        to_right = jnp.logical_and(jnp.logical_not(in_left), right_valid)
        for part in range(2):
            turned = pltpu.roll(grads[slot][part] + part_ref[slot, part], shift, 1)
            grad_ref[left, part, rows, :] += jnp.where(to_left, turned, 0.0)
            grad_ref[right, part, rows, :] += jnp.where(to_right, turned, 0.0)


def run_first(offsets, counts, blocks, probe, patterns, tables):
    modes, _, width, _ = probe.shape
    half = modes // 2
    slots = patterns.shape[2]
    vmem = pl.BlockSpec(memory_space=pltpu.VMEM)
    images = lambda *lead: jax.ShapeDtypeStruct((*lead, 2, width, width), jnp.float32)
    return pl.pallas_call(
        first_kernel,
        out_shape=(images(half), images(slots), images(slots, half), images(slots)),
        in_specs=[
            pl.BlockSpec(memory_space=pltpu.HBM),
            pl.BlockSpec(memory_space=pltpu.SMEM),
        ]
        + [vmem] * 9,
        out_specs=(vmem,) * 4,
        scratch_shapes=[
            pltpu.SMEM(offsets.shape, offsets.dtype),
            pltpu.SemaphoreType.DMA,
            pltpu.VMEM((2, 2, 3 * width, width), jnp.float32),
        ],
        cost_estimate=pl.CostEstimate(
            flops=slots * modes * 3 * 3 * 8 * width**3,
            bytes_accessed=40 * width * width * 4,
            transcendentals=0,
        ),
        compiler_params=pltpu.CompilerParams(vmem_limit_bytes=16 << 20),
        name="first",
    )(offsets, counts, *blocks, probe, patterns, tables)


def run_second(offsets, probe, tables, window, kept, part):
    modes, _, width, _ = probe.shape
    half = modes // 2
    slots = window.shape[0]
    vmem = pl.BlockSpec(memory_space=pltpu.VMEM)
    return pl.pallas_call(
        second_kernel,
        out_shape=(
            jax.ShapeDtypeStruct((half, 2, width, width), jnp.float32),
            jax.ShapeDtypeStruct((2, 2, 3 * width, width), jnp.float32),
        ),
        in_specs=[pl.BlockSpec(memory_space=pltpu.HBM)] + [vmem] * 5,
        out_specs=(vmem,) * 2,
        scratch_shapes=[
            pltpu.SMEM(offsets.shape, offsets.dtype),
            pltpu.SemaphoreType.DMA,
        ],
        cost_estimate=pl.CostEstimate(
            flops=slots * modes * 3 * 8 * width**3,
            bytes_accessed=30 * width * width * 4,
            transcendentals=0,
        ),
        compiler_params=pltpu.CompilerParams(vmem_limit_bytes=16 << 20),
        name="second",
    )(offsets, probe, tables, window, kept, part)


def total_kernel(parts_ref, out_ref):
    total = parts_ref[0]
    for index in range(1, parts_ref.shape[0]):
        total = total + parts_ref[index]
    for index in range(parts_ref.shape[0]):
        out_ref[index] = total


def strips_kernel(grads_ref, got_ref, middle_ref, near_ref, far_ref):
    width = got_ref.shape[-1]
    odd = lax.rem(lax.axis_index("row"), 2)
    near_at = pl.multiple_of((1 - odd) * (2 * width), width)
    far_at = pl.multiple_of(odd * (2 * width), width)
    for out_ref, place in ((middle_ref, width), (near_ref, near_at), (far_ref, far_at)):
        rows = pl.ds(place, width)
        out_ref[...] = grads_ref[0, :, rows, :] + got_ref[:, rows, :]


def object_kernel(own_ref, middle_ref, near_ref, far_ref, weight_ref, out_ref):
    weight = weight_ref[...]
    grad = (middle_ref[...] + near_ref[...] + far_ref[...]).reshape(-1, *weight.shape)
    out = own_ref[...].reshape(grad.shape) - object_rate * (grad / weight)
    out_ref[...] = out.reshape(own_ref.shape)


def probe_kernel(tile_total, probe_ref, mine_ref, other_ref, out_ref):
    half = mine_ref.shape[0]
    core = lax.axis_index("col")
    for part_ref, which in ((mine_ref, core), (other_ref, 1 - core)):
        modes = pl.ds(which * half, half)
        out_ref[modes] = probe_ref[modes] - probe_rate * part_ref[...] / tile_total


def in_vmem(kernel, shapes, *operands):
    vmem = pl.BlockSpec(memory_space=pltpu.VMEM)
    out = tuple(jax.ShapeDtypeStruct(shape, jnp.float32) for shape in shapes)
    size = sum(a.size for a in out + operands)
    return pl.pallas_call(
        kernel,
        out_shape=out if len(out) > 1 else out[0],
        in_specs=[vmem] * len(operands),
        out_specs=(vmem,) * len(out) if len(out) > 1 else vmem,
        cost_estimate=pl.CostEstimate(flops=size, bytes_accessed=4 * size, transcendentals=0),
        compiler_params=pltpu.CompilerParams(vmem_limit_bytes=8 << 20),
    )(*operands)


def member_order(count):
    pairs = list(range(count // 2))
    order = []
    for at in pairs[0::2][::-1] + pairs[1::2][::-1]:
        order.extend((2 * at + 1, 2 * at))
    return order


def body(object_field, probe, patterns, offsets, counts):
    row_total = lax.axis_size("row")
    tile_total = row_total * lax.axis_size("col")
    modes, _, width, _ = probe.shape
    half = modes // 2

    pair = [(0, 1), (1, 0)]
    near = [(i, i ^ 1) for i in range(row_total)]
    far = [(i, i + 1) for i in range(1, row_total - 1, 2)]
    far = far + [(target, source) for source, target in far]

    near_block = lax.ppermute(object_field, "row", near)
    far_block = lax.ppermute(object_field, "row", far)
    own_pair = lax.ppermute(object_field, "col", pair)
    near_pair = lax.ppermute(near_block, "col", pair)
    far_pair = lax.ppermute(far_block, "col", pair)
    probe_here, patterns_here, own, tables, weight = stage(
        probe, patterns, object_field, jnp.asarray(host_tables(width))
    )
    blocks = (own, own_pair, near_block, near_pair, far_block, far_pair)
    offsets = pltpu.with_memory_space_constraint(offsets, pltpu.HBM)
    send_probe, window, kept, part = run_first(
        offsets, counts, blocks, probe_here, patterns_here, tables
    )
    got_probe = lax.ppermute(send_probe, "col", pair)
    keep_probe, grads = run_second(offsets, probe_here, tables, window, kept, part)
    got_grad = lax.ppermute(grads[1], "col", pair)

    members = [member_order(row_total)]
    mine = (keep_probe + got_probe).reshape(row_total, -1, width)
    mine = lax.all_to_all(mine, "row", 0, 0, tiled=True, axis_index_groups=members)
    mine = in_vmem(total_kernel, [mine.shape], mine)
    block = own.shape
    middle, near_strip, far_strip = in_vmem(
        strips_kernel, [block, block, block], grads, got_grad
    )
    near_strip = lax.ppermute(near_strip, "row", near)
    far_strip = lax.ppermute(far_strip, "row", far)
    mine = lax.all_to_all(mine, "row", 0, 0, tiled=True, axis_index_groups=members)
    mine = mine.reshape(half, 2, width, width)
    other = lax.ppermute(mine, "col", pair)
    object_field = in_vmem(
        object_kernel, [block], own, middle, near_strip, far_strip, weight
    )
    probe = in_vmem(
        functools.partial(probe_kernel, tile_total), [probe.shape], probe_here, mine, other
    )
    return (object_field, probe)


def solution(mesh):
    placed = (
        P(None, ("tilt", "row"), "col"),
        P("tilt", None, None, None),
        P(("tilt", "row"), "col", None, None, None),
        P(("tilt", "row"), "col", None, None),
        P(("tilt", "row"), "col"),
    )

    return jax.shard_map(
        body,
        mesh=mesh,
        in_specs=placed,
        out_specs=(P(None, ("tilt", "row"), "col"), P("tilt", None, None, None)),
        check_vma=False,
    )
```

```python
import functools

import jax
import jax.numpy as jnp
import numpy as np
from jax import lax
from jax.experimental import pallas as pl
from jax.experimental.pallas import tpu as pltpu
from jax.sharding import PartitionSpec as P


object_rate = 1.0
probe_rate = 1.0
epsilon = 1e-06


def split(value):
    high = value.astype(jnp.bfloat16)
    low = (value - high.astype(jnp.float32)).astype(jnp.bfloat16)
    return high, low


def host_tables(length):
    counter = np.arange(length)
    angle = -2.0 * np.pi / length * (counter[:, None] * counter[None, :] % length)
    cosine = (np.cos(angle) / np.sqrt(length)).astype(np.float32)
    sine = (np.sin(angle) / np.sqrt(length)).astype(np.float32)
    plain = np.block([[cosine, sine], [-sine, cosine]])
    conj = np.block([[cosine, -sine], [sine, cosine]])
    both = np.stack([plain, conj])
    high = both.astype(jnp.bfloat16)
    low = (both - high.astype(np.float32)).astype(jnp.bfloat16)
    return np.concatenate([high, low])


def stage_kernel(count, *refs):
    sources, targets, power_of = refs[:count], refs[count : 2 * count], refs[count]
    weight_ref, sems = refs[2 * count :]
    copies = [
        pltpu.make_async_copy(source, target, sems.at[index])
        for index, (source, target) in enumerate(zip(sources, targets))
    ]
    for copy in copies:
        copy.start()
    for copy in copies:
        copy.wait()
    power = jnp.zeros(power_of.shape[2:], jnp.float32)
    for k in range(power_of.shape[0]):
        power = power + power_of[k, 0] * power_of[k, 0] + power_of[k, 1] * power_of[k, 1]
    weight_ref[...] = jnp.full(weight_ref.shape, jnp.max(power) + epsilon, jnp.float32)


def stage(probe, *others):
    arrays = tuple(
        pltpu.with_memory_space_constraint(a, pltpu.HBM) for a in (probe,) + others
    )
    count = len(arrays)
    return pl.pallas_call(
        lambda *refs: stage_kernel(count, *refs),
        out_shape=tuple(jax.ShapeDtypeStruct(a.shape, a.dtype) for a in arrays)
        + (jax.ShapeDtypeStruct((8, probe.shape[-1]), jnp.float32),),
        in_specs=[pl.BlockSpec(memory_space=pltpu.HBM)] * count,
        out_specs=(pl.BlockSpec(memory_space=pltpu.VMEM),) * (count + 1),
        scratch_shapes=[pltpu.SemaphoreType.DMA((count,))],
        cost_estimate=pl.CostEstimate(
            flops=8 * probe.size,
            bytes_accessed=sum(2 * a.size * a.dtype.itemsize for a in arrays),
            transcendentals=0,
        ),
        compiler_params=pltpu.CompilerParams(vmem_limit_bytes=8 << 20),
        name="stage",
    )(*arrays)


def product(pieces, tables_ref, which, on_left):
    width = pieces[0][0].shape[0]
    inner, outer = (0, 1) if on_left else (1, 0)
    value = jnp.concatenate([jnp.concatenate(piece, axis=inner) for piece in pieces], axis=outer)
    high, low = split(value)
    if on_left:
        table = jnp.concatenate(
            [tables_ref[1 - which], tables_ref[1 - which], tables_ref[3 - which]], axis=1
        )
        out = jnp.dot(
            table, jnp.concatenate([high, low, high], axis=0), preferred_element_type=jnp.float32
        )
    else:
        table = jnp.concatenate(
            [tables_ref[which], tables_ref[2 + which], tables_ref[which]], axis=0
        )
        out = jnp.dot(
            jnp.concatenate([high, high, low], axis=1), table, preferred_element_type=jnp.float32
        )
    found = []
    for index in range(len(pieces)):
        part = lax.slice_in_dim(out, index * width, (index + 1) * width, axis=outer)
        found.append(
            (
                lax.slice_in_dim(part, 0, width, axis=inner),
                lax.slice_in_dim(part, width, 2 * width, axis=inner),
            )
        )
    return found


def in_groups(value, size, *rest):
    found = []
    for at in range(0, len(value), size):
        found += product(value[at : at + size], *rest)
    return found


def columns_of(corner_x, width, core):
    column = corner_x // width
    shift = corner_x - column * width
    pair_column = 2 - 2 * core
    found = []
    for place in (column, column + 1):
        is_pair = (place == pair_column).astype(jnp.int32)
        valid = jnp.logical_or(place == 1, place == pair_column)
        found.append((is_pair, valid))
    lane = lax.broadcasted_iota(jnp.int32, (width, width), 1)
    in_left = lane >= shift
    return shift, in_left, found


def first_kernel(
    offsets_ref,
    counts_ref,
    own_ref,
    own_pair_ref,
    near_ref,
    near_pair_ref,
    far_ref,
    far_pair_ref,
    probe_ref,
    patterns_ref,
    tables_ref,
    send_probe_ref,
    window_ref,
    kept_ref,
    grad_ref,
    frame,
):
    modes = probe_ref.shape[0]
    width = probe_ref.shape[-1]
    slots = patterns_ref.shape[2]
    half = modes // 2
    core = lax.axis_index("col")
    odd = lax.rem(lax.axis_index("row"), 2)
    near_at = pl.multiple_of((1 - odd) * (2 * width), width)
    far_at = pl.multiple_of(odd * (2 * width), width)
    for index, (own, near, far) in enumerate(
        ((own_ref, near_ref, far_ref), (own_pair_ref, near_pair_ref, far_pair_ref))
    ):
        frame[index, :, pl.ds(width, width), :] = own[...]
        frame[index, :, pl.ds(near_at, width), :] = near[...]
        frame[index, :, pl.ds(far_at, width), :] = far[...]

    mine = core * half
    order = [half - mine + k for k in range(half)] + [mine + k for k in range(half)]
    windows = []
    for slot in range(slots):
        rows = pl.ds(offsets_ref[0, 0, slot, 0], width)
        shift, in_left, blocks = columns_of(offsets_ref[0, 0, slot, 1], width, core)
        back_shift = lax.rem(width - shift, width)
        (left, left_valid), (right, right_valid) = blocks
        valid = jnp.logical_or(
            jnp.logical_and(in_left, left_valid),
            jnp.logical_and(jnp.logical_not(in_left), right_valid),
        )
        window = []
        for part in range(2):
            both = jnp.where(in_left, frame[left, part, rows, :], frame[right, part, rows, :])
            value = pltpu.roll(jnp.where(valid, both, 0.0), back_shift, 1)
            window_ref[slot, part] = value
            window.append(value)
        windows.append(window)

    values = []
    for win_re, win_im in windows:
        exits = []
        for k in order:
            probe_re, probe_im = probe_ref[k, 0], probe_ref[k, 1]
            exits.append(
                (
                    probe_re * win_re - probe_im * win_im,
                    probe_re * win_im + probe_im * win_re,
                )
            )
        values.append(exits)
    values = [in_groups(value, 2, tables_ref, 0, False) for value in values]
    values = [in_groups(value, 4, tables_ref, 0, True) for value in values]
    backs = []
    for slot, far in enumerate(values):
        live = (slot < counts_ref[0, 0]).astype(jnp.float32)
        intensity = sum(re * re + im * im for re, im in far)
        misfit = (intensity - patterns_ref[0, 0, slot]) * live
        for k in range(half):
            for part in range(2):
                kept_ref[slot, k, part] = misfit * far[half + k][part]
        back = [(misfit * re, misfit * im) for re, im in far[:half]]
        backs.append(in_groups(back, 2, tables_ref, 1, True))
    backs = [in_groups(back, 2, tables_ref, 1, False) for back in backs]
    grads = combine(backs, probe_ref, order[:half], windows, send_probe_ref)
    for slot in range(slots):
        for part in range(2):
            grad_ref[slot, part] = grads[slot][part]


def combine(backs, probe_ref, order, windows, term_ref):
    grads = [[jnp.zeros_like(part) for part in window] for window in windows]
    for index, k in enumerate(order):
        probe_re, probe_im = probe_ref[k, 0], probe_ref[k, 1]
        term_re, term_im = 0.0, 0.0
        for slot, (win_re, win_im) in enumerate(windows):
            back_re, back_im = backs[slot][index]
            grads[slot][0] += probe_re * back_re + probe_im * back_im
            grads[slot][1] += probe_re * back_im - probe_im * back_re
            term_re += win_re * back_re + win_im * back_im
            term_im += win_re * back_im - win_im * back_re
        term_ref[index, 0] = term_re
        term_ref[index, 1] = term_im
    return grads


def second_kernel(
    offsets_ref,
    probe_ref,
    tables_ref,
    window_ref,
    kept_ref,
    part_ref,
    keep_probe_ref,
    grad_ref,
):
    modes = probe_ref.shape[0]
    width = probe_ref.shape[-1]
    slots = window_ref.shape[0]
    half = modes // 2
    core = lax.axis_index("col")
    order = [core * half + k for k in range(half)]
    grad_ref[...] = jnp.zeros_like(grad_ref)
    backs = [
        [(kept_ref[slot, k, 0], kept_ref[slot, k, 1]) for k in range(half)]
        for slot in range(slots)
    ]
    windows = [[window_ref[slot, 0], window_ref[slot, 1]] for slot in range(slots)]
    backs = [in_groups(back, 2, tables_ref, 1, True) for back in backs]
    backs = [in_groups(back, 2, tables_ref, 1, False) for back in backs]
    grads = combine(backs, probe_ref, order, windows, keep_probe_ref)
    for slot in range(slots):
        rows = pl.ds(offsets_ref[0, 0, slot, 0], width)
        shift, in_left, blocks = columns_of(offsets_ref[0, 0, slot, 1], width, core)
        (left, left_valid), (right, right_valid) = blocks
        to_left = jnp.logical_and(in_left, left_valid)
        to_right = jnp.logical_and(jnp.logical_not(in_left), right_valid)
        for part in range(2):
            turned = pltpu.roll(grads[slot][part] + part_ref[slot, part], shift, 1)
            grad_ref[left, part, rows, :] += jnp.where(to_left, turned, 0.0)
            grad_ref[right, part, rows, :] += jnp.where(to_right, turned, 0.0)


def run_first(offsets, counts, blocks, probe, patterns, tables):
    modes, _, width, _ = probe.shape
    half = modes // 2
    slots = patterns.shape[2]
    vmem = pl.BlockSpec(memory_space=pltpu.VMEM)
    images = lambda *lead: jax.ShapeDtypeStruct((*lead, 2, width, width), jnp.float32)
    return pl.pallas_call(
        first_kernel,
        out_shape=(images(half), images(slots), images(slots, half), images(slots)),
        in_specs=[
            pl.BlockSpec(memory_space=pltpu.VMEM),
            pl.BlockSpec(memory_space=pltpu.SMEM),
        ]
        + [vmem] * 9,
        out_specs=(vmem,) * 4,
        scratch_shapes=[
            pltpu.VMEM((2, 2, 3 * width, width), jnp.float32),
        ],
        cost_estimate=pl.CostEstimate(
            flops=slots * modes * 3 * 3 * 8 * width**3,
            bytes_accessed=40 * width * width * 4,
            transcendentals=0,
        ),
        compiler_params=pltpu.CompilerParams(vmem_limit_bytes=16 << 20),
        name="first",
    )(offsets, counts, *blocks, probe, patterns, tables)


def run_second(offsets, probe, tables, window, kept, part):
    modes, _, width, _ = probe.shape
    half = modes // 2
    slots = window.shape[0]
    vmem = pl.BlockSpec(memory_space=pltpu.VMEM)
    return pl.pallas_call(
        second_kernel,
        out_shape=(
            jax.ShapeDtypeStruct((half, 2, width, width), jnp.float32),
            jax.ShapeDtypeStruct((2, 2, 3 * width, width), jnp.float32),
        ),
        in_specs=[vmem] * 6,
        out_specs=(vmem,) * 2,
        scratch_shapes=[
        ],
        cost_estimate=pl.CostEstimate(
            flops=slots * modes * 3 * 8 * width**3,
            bytes_accessed=30 * width * width * 4,
            transcendentals=0,
        ),
        compiler_params=pltpu.CompilerParams(vmem_limit_bytes=16 << 20),
        name="second",
    )(offsets, probe, tables, window, kept, part)


def total_kernel(parts_ref, out_ref):
    total = parts_ref[0]
    for index in range(1, parts_ref.shape[0]):
        total = total + parts_ref[index]
    for index in range(parts_ref.shape[0]):
        out_ref[index] = total


def strips_kernel(grads_ref, got_ref, middle_ref, near_ref, far_ref):
    width = got_ref.shape[-1]
    odd = lax.rem(lax.axis_index("row"), 2)
    near_at = pl.multiple_of((1 - odd) * (2 * width), width)
    far_at = pl.multiple_of(odd * (2 * width), width)
    for out_ref, place in ((middle_ref, width), (near_ref, near_at), (far_ref, far_at)):
        rows = pl.ds(place, width)
        out_ref[...] = grads_ref[0, :, rows, :] + got_ref[:, rows, :]


def object_kernel(own_ref, middle_ref, near_ref, far_ref, weight_ref, out_ref):
    weight = weight_ref[...]
    grad = (middle_ref[...] + near_ref[...] + far_ref[...]).reshape(-1, *weight.shape)
    out = own_ref[...].reshape(grad.shape) - object_rate * (grad / weight)
    out_ref[...] = out.reshape(own_ref.shape)


def probe_kernel(tile_total, probe_ref, mine_ref, other_ref, out_ref):
    half = mine_ref.shape[0]
    core = lax.axis_index("col")
    for part_ref, which in ((mine_ref, core), (other_ref, 1 - core)):
        modes = pl.ds(which * half, half)
        out_ref[modes] = probe_ref[modes] - probe_rate * part_ref[...] / tile_total


def in_vmem(kernel, shapes, *operands):
    vmem = pl.BlockSpec(memory_space=pltpu.VMEM)
    out = tuple(jax.ShapeDtypeStruct(shape, jnp.float32) for shape in shapes)
    size = sum(a.size for a in out + operands)
    return pl.pallas_call(
        kernel,
        out_shape=out if len(out) > 1 else out[0],
        in_specs=[vmem] * len(operands),
        out_specs=(vmem,) * len(out) if len(out) > 1 else vmem,
        cost_estimate=pl.CostEstimate(flops=size, bytes_accessed=4 * size, transcendentals=0),
        compiler_params=pltpu.CompilerParams(vmem_limit_bytes=8 << 20),
    )(*operands)


def member_order(count):
    pairs = list(range(count // 2))
    order = []
    for at in pairs[0::2][::-1] + pairs[1::2][::-1]:
        order.extend((2 * at + 1, 2 * at))
    return order


def body(object_field, probe, patterns, offsets, counts):
    row_total = lax.axis_size("row")
    tile_total = row_total * lax.axis_size("col")
    modes, _, width, _ = probe.shape
    half = modes // 2

    pair = [(0, 1), (1, 0)]
    near = [(i, i ^ 1) for i in range(row_total)]
    far = [(i, i + 1) for i in range(1, row_total - 1, 2)]
    far = far + [(target, source) for source, target in far]

    near_block = lax.ppermute(object_field, "row", near)
    far_block = lax.ppermute(object_field, "row", far)
    own_pair = lax.ppermute(object_field, "col", pair)
    near_pair = lax.ppermute(near_block, "col", pair)
    far_pair = lax.ppermute(far_block, "col", pair)
    probe_here, patterns_here, own, tables, offsets, weight = stage(
        probe, patterns, object_field, jnp.asarray(host_tables(width)), offsets
    )
    blocks = (own, own_pair, near_block, near_pair, far_block, far_pair)
    send_probe, window, kept, part = run_first(
        offsets, counts, blocks, probe_here, patterns_here, tables
    )
    got_probe = lax.ppermute(send_probe, "col", pair)
    keep_probe, grads = run_second(offsets, probe_here, tables, window, kept, part)
    got_grad = lax.ppermute(grads[1], "col", pair)

    members = [member_order(row_total)]
    mine = (keep_probe + got_probe).reshape(row_total, -1, width)
    mine = lax.all_to_all(mine, "row", 0, 0, tiled=True, axis_index_groups=members)
    mine = in_vmem(total_kernel, [mine.shape], mine)
    block = own.shape
    middle, near_strip, far_strip = in_vmem(
        strips_kernel, [block, block, block], grads, got_grad
    )
    near_strip = lax.ppermute(near_strip, "row", near)
    far_strip = lax.ppermute(far_strip, "row", far)
    mine = lax.all_to_all(mine, "row", 0, 0, tiled=True, axis_index_groups=members)
    mine = mine.reshape(half, 2, width, width)
    other = lax.ppermute(mine, "col", pair)
    object_field = in_vmem(
        object_kernel, [block], own, middle, near_strip, far_strip, weight
    )
    probe = in_vmem(
        functools.partial(probe_kernel, tile_total), [probe.shape], probe_here, mine, other
    )
    return (object_field, probe)


def solution(mesh):
    placed = (
        P(None, ("tilt", "row"), "col"),
        P("tilt", None, None, None),
        P(("tilt", "row"), "col", None, None, None),
        P(("tilt", "row"), "col", None, None),
        P(("tilt", "row"), "col"),
    )

    return jax.shard_map(
        body,
        mesh=mesh,
        in_specs=placed,
        out_specs=(P(None, ("tilt", "row"), "col"), P("tilt", None, None, None)),
        check_vma=False,
    )
```

```python
import functools

import jax
import jax.numpy as jnp
import numpy as np
from jax import lax
from jax.experimental import pallas as pl
from jax.experimental.pallas import tpu as pltpu
from jax.sharding import PartitionSpec as P


object_rate = 1.0
probe_rate = 1.0
epsilon = 1e-06


def split(value):
    high = value.astype(jnp.bfloat16)
    low = (value - high.astype(jnp.float32)).astype(jnp.bfloat16)
    return high, low


def host_tables(length):
    counter = np.arange(length)
    angle = -2.0 * np.pi / length * (counter[:, None] * counter[None, :] % length)
    cosine = (np.cos(angle) / np.sqrt(length)).astype(np.float32)
    sine = (np.sin(angle) / np.sqrt(length)).astype(np.float32)
    plain = np.block([[cosine, sine], [-sine, cosine]])
    conj = np.block([[cosine, -sine], [sine, cosine]])
    both = np.stack([plain, conj])
    high = both.astype(jnp.bfloat16)
    low = (both - high.astype(np.float32)).astype(jnp.bfloat16)
    return np.concatenate([high, low])


def stage_kernel(count, *refs):
    sources, targets, power_of = refs[:count], refs[count : 2 * count], refs[count]
    weight_ref, sems = refs[2 * count :]
    copies = [
        pltpu.make_async_copy(source, target, sems.at[index])
        for index, (source, target) in enumerate(zip(sources, targets))
    ]
    for copy in copies:
        copy.start()
    for copy in copies:
        copy.wait()
    power = jnp.zeros(power_of.shape[2:], jnp.float32)
    for k in range(power_of.shape[0]):
        power = power + power_of[k, 0] * power_of[k, 0] + power_of[k, 1] * power_of[k, 1]
    weight_ref[...] = jnp.full(weight_ref.shape, jnp.max(power) + epsilon, jnp.float32)


def stage(probe, *others):
    arrays = tuple(
        pltpu.with_memory_space_constraint(a, pltpu.HBM) for a in (probe,) + others
    )
    count = len(arrays)
    return pl.pallas_call(
        lambda *refs: stage_kernel(count, *refs),
        out_shape=tuple(jax.ShapeDtypeStruct(a.shape, a.dtype) for a in arrays)
        + (jax.ShapeDtypeStruct((8, probe.shape[-1]), jnp.float32),),
        in_specs=[pl.BlockSpec(memory_space=pltpu.HBM)] * count,
        out_specs=(pl.BlockSpec(memory_space=pltpu.VMEM),) * (count + 1),
        scratch_shapes=[pltpu.SemaphoreType.DMA((count,))],
        cost_estimate=pl.CostEstimate(
            flops=8 * probe.size,
            bytes_accessed=sum(2 * a.size * a.dtype.itemsize for a in arrays),
            transcendentals=0,
        ),
        compiler_params=pltpu.CompilerParams(vmem_limit_bytes=8 << 20),
        name="stage",
    )(*arrays)


def product(pieces, tables_ref, which, on_left):
    width = pieces[0][0].shape[0]
    inner, outer = (0, 1) if on_left else (1, 0)
    value = jnp.concatenate([jnp.concatenate(piece, axis=inner) for piece in pieces], axis=outer)
    high, low = split(value)
    if on_left:
        table = jnp.concatenate(
            [tables_ref[1 - which], tables_ref[1 - which], tables_ref[3 - which]], axis=1
        )
        out = jnp.dot(
            table, jnp.concatenate([high, low, high], axis=0), preferred_element_type=jnp.float32
        )
    else:
        table = jnp.concatenate(
            [tables_ref[which], tables_ref[2 + which], tables_ref[which]], axis=0
        )
        out = jnp.dot(
            jnp.concatenate([high, high, low], axis=1), table, preferred_element_type=jnp.float32
        )
    found = []
    for index in range(len(pieces)):
        part = lax.slice_in_dim(out, index * width, (index + 1) * width, axis=outer)
        found.append(
            (
                lax.slice_in_dim(part, 0, width, axis=inner),
                lax.slice_in_dim(part, width, 2 * width, axis=inner),
            )
        )
    return found


def in_groups(value, size, *rest):
    found = []
    for at in range(0, len(value), size):
        found += product(value[at : at + size], *rest)
    return found


def columns_of(corner_x, width, core):
    column = corner_x // width
    shift = corner_x - column * width
    pair_column = 2 - 2 * core
    found = []
    for place in (column, column + 1):
        is_pair = (place == pair_column).astype(jnp.int32)
        valid = jnp.logical_or(place == 1, place == pair_column)
        found.append((is_pair, valid))
    lane = lax.broadcasted_iota(jnp.int32, (width, width), 1)
    in_left = lane >= shift
    return shift, in_left, found


def first_kernel(
    offsets_ref,
    counts_ref,
    own_ref,
    own_pair_ref,
    near_ref,
    near_pair_ref,
    far_ref,
    far_pair_ref,
    probe_ref,
    patterns_ref,
    tables_ref,
    send_probe_ref,
    window_ref,
    kept_ref,
    grad_ref,
    frame,
):
    modes = probe_ref.shape[0]
    width = probe_ref.shape[-1]
    slots = patterns_ref.shape[2]
    half = modes // 2
    core = lax.axis_index("col")
    odd = lax.rem(lax.axis_index("row"), 2)
    near_at = pl.multiple_of((1 - odd) * (2 * width), width)
    far_at = pl.multiple_of(odd * (2 * width), width)
    for index, (own, near, far) in enumerate(
        ((own_ref, near_ref, far_ref), (own_pair_ref, near_pair_ref, far_pair_ref))
    ):
        frame[index, :, pl.ds(width, width), :] = own[...]
        frame[index, :, pl.ds(near_at, width), :] = near[...]
        frame[index, :, pl.ds(far_at, width), :] = far[...]

    mine = core * half
    order = [half - mine + k for k in range(half)] + [mine + k for k in range(half)]
    windows = []
    for slot in range(slots):
        rows = pl.ds(offsets_ref[0, 0, slot, 0], width)
        shift, in_left, blocks = columns_of(offsets_ref[0, 0, slot, 1], width, core)
        back_shift = lax.rem(width - shift, width)
        (left, left_valid), (right, right_valid) = blocks
        valid = jnp.logical_or(
            jnp.logical_and(in_left, left_valid),
            jnp.logical_and(jnp.logical_not(in_left), right_valid),
        )
        window = []
        for part in range(2):
            both = jnp.where(in_left, frame[left, part, rows, :], frame[right, part, rows, :])
            value = pltpu.roll(jnp.where(valid, both, 0.0), back_shift, 1)
            window_ref[slot, part] = value
            window.append(value)
        windows.append(window)

    values = []
    for win_re, win_im in windows:
        exits = []
        for k in order:
            probe_re, probe_im = probe_ref[k, 0], probe_ref[k, 1]
            exits.append(
                (
                    probe_re * win_re - probe_im * win_im,
                    probe_re * win_im + probe_im * win_re,
                )
            )
        values.append(exits)
    values = [in_groups(value, 2, tables_ref, 0, False) for value in values]
    values = [in_groups(value, 4, tables_ref, 0, True) for value in values]
    backs = []
    for slot, far in enumerate(values):
        live = (slot < counts_ref[0, 0]).astype(jnp.float32)
        intensity = sum(re * re + im * im for re, im in far)
        misfit = (intensity - patterns_ref[0, 0, slot]) * live
        for k in range(half):
            for part in range(2):
                kept_ref[slot, k, part] = misfit * far[half + k][part]
        backs.append([(misfit * re, misfit * im) for re, im in far[:half]])
    backs = [in_groups(back, 2, tables_ref, 1, True) for back in backs]
    backs = [in_groups(back, 2, tables_ref, 1, False) for back in backs]
    grads = combine(backs, probe_ref, order[:half], windows, send_probe_ref)
    for slot in range(slots):
        for part in range(2):
            grad_ref[slot, part] = grads[slot][part]


def combine(backs, probe_ref, order, windows, term_ref):
    grads = [[jnp.zeros_like(part) for part in window] for window in windows]
    for index, k in enumerate(order):
        probe_re, probe_im = probe_ref[k, 0], probe_ref[k, 1]
        term_re, term_im = 0.0, 0.0
        for slot, (win_re, win_im) in enumerate(windows):
            back_re, back_im = backs[slot][index]
            grads[slot][0] += probe_re * back_re + probe_im * back_im
            grads[slot][1] += probe_re * back_im - probe_im * back_re
            term_re += win_re * back_re + win_im * back_im
            term_im += win_re * back_im - win_im * back_re
        term_ref[index, 0] = term_re
        term_ref[index, 1] = term_im
    return grads


def second_kernel(
    offsets_ref,
    probe_ref,
    tables_ref,
    window_ref,
    kept_ref,
    part_ref,
    keep_probe_ref,
    grad_ref,
):
    modes = probe_ref.shape[0]
    width = probe_ref.shape[-1]
    slots = window_ref.shape[0]
    half = modes // 2
    core = lax.axis_index("col")
    order = [core * half + k for k in range(half)]
    grad_ref[...] = jnp.zeros_like(grad_ref)
    backs = [
        [(kept_ref[slot, k, 0], kept_ref[slot, k, 1]) for k in range(half)]
        for slot in range(slots)
    ]
    windows = [[window_ref[slot, 0], window_ref[slot, 1]] for slot in range(slots)]
    backs = [in_groups(back, 2, tables_ref, 1, True) for back in backs]
    backs = [in_groups(back, 2, tables_ref, 1, False) for back in backs]
    grads = combine(backs, probe_ref, order, windows, keep_probe_ref)
    for slot in range(slots):
        rows = pl.ds(offsets_ref[0, 0, slot, 0], width)
        shift, in_left, blocks = columns_of(offsets_ref[0, 0, slot, 1], width, core)
        (left, left_valid), (right, right_valid) = blocks
        to_left = jnp.logical_and(in_left, left_valid)
        to_right = jnp.logical_and(jnp.logical_not(in_left), right_valid)
        for part in range(2):
            turned = pltpu.roll(grads[slot][part] + part_ref[slot, part], shift, 1)
            grad_ref[left, part, rows, :] += jnp.where(to_left, turned, 0.0)
            grad_ref[right, part, rows, :] += jnp.where(to_right, turned, 0.0)


def run_first(offsets, counts, blocks, probe, patterns, tables):
    modes, _, width, _ = probe.shape
    half = modes // 2
    slots = patterns.shape[2]
    vmem = pl.BlockSpec(memory_space=pltpu.VMEM)
    images = lambda *lead: jax.ShapeDtypeStruct((*lead, 2, width, width), jnp.float32)
    return pl.pallas_call(
        first_kernel,
        out_shape=(images(half), images(slots), images(slots, half), images(slots)),
        in_specs=[
            pl.BlockSpec(memory_space=pltpu.VMEM),
            pl.BlockSpec(memory_space=pltpu.SMEM),
        ]
        + [vmem] * 9,
        out_specs=(vmem,) * 4,
        scratch_shapes=[
            pltpu.VMEM((2, 2, 3 * width, width), jnp.float32),
        ],
        cost_estimate=pl.CostEstimate(
            flops=slots * modes * 3 * 3 * 8 * width**3,
            bytes_accessed=40 * width * width * 4,
            transcendentals=0,
        ),
        compiler_params=pltpu.CompilerParams(vmem_limit_bytes=16 << 20),
        name="first",
    )(offsets, counts, *blocks, probe, patterns, tables)


def run_second(offsets, probe, tables, window, kept, part):
    modes, _, width, _ = probe.shape
    half = modes // 2
    slots = window.shape[0]
    vmem = pl.BlockSpec(memory_space=pltpu.VMEM)
    return pl.pallas_call(
        second_kernel,
        out_shape=(
            jax.ShapeDtypeStruct((half, 2, width, width), jnp.float32),
            jax.ShapeDtypeStruct((2, 2, 3 * width, width), jnp.float32),
        ),
        in_specs=[vmem] * 6,
        out_specs=(vmem,) * 2,
        scratch_shapes=[
        ],
        cost_estimate=pl.CostEstimate(
            flops=slots * modes * 3 * 8 * width**3,
            bytes_accessed=30 * width * width * 4,
            transcendentals=0,
        ),
        compiler_params=pltpu.CompilerParams(vmem_limit_bytes=16 << 20),
        name="second",
    )(offsets, probe, tables, window, kept, part)


def total_kernel(parts_ref, out_ref):
    total = parts_ref[0]
    for index in range(1, parts_ref.shape[0]):
        total = total + parts_ref[index]
    for index in range(parts_ref.shape[0]):
        out_ref[index] = total


def strips_kernel(grads_ref, got_ref, middle_ref, near_ref, far_ref):
    width = got_ref.shape[-1]
    odd = lax.rem(lax.axis_index("row"), 2)
    near_at = pl.multiple_of((1 - odd) * (2 * width), width)
    far_at = pl.multiple_of(odd * (2 * width), width)
    for out_ref, place in ((middle_ref, width), (near_ref, near_at), (far_ref, far_at)):
        rows = pl.ds(place, width)
        out_ref[...] = grads_ref[0, :, rows, :] + got_ref[:, rows, :]


def object_kernel(own_ref, middle_ref, near_ref, far_ref, weight_ref, out_ref):
    weight = weight_ref[...]
    grad = (middle_ref[...] + near_ref[...] + far_ref[...]).reshape(-1, *weight.shape)
    out = own_ref[...].reshape(grad.shape) - object_rate * (grad / weight)
    out_ref[...] = out.reshape(own_ref.shape)


def probe_kernel(tile_total, is_mine, probe_ref, part_ref, *refs):
    out_ref, staged, sems = refs[-3:]
    half = part_ref.shape[0]
    core = lax.axis_index("col")
    first = half * (core if is_mine else 1 - core)
    copies = []
    for k in range(half):
        staged[k] = probe_ref[first + k] - probe_rate * part_ref[k] / tile_total
        copies.append(pltpu.make_async_copy(staged.at[k], out_ref.at[first + k], sems.at[k]))
        copies[-1].start()
    for copy in copies:
        copy.wait()


def put_half(tile_total, is_mine, probe, part, *buffer):
    half = part.shape[0]
    vmem, hbm = (pl.BlockSpec(memory_space=space) for space in (pltpu.VMEM, pltpu.HBM))
    return pl.pallas_call(
        functools.partial(probe_kernel, tile_total, is_mine),
        out_shape=jax.ShapeDtypeStruct(probe.shape, probe.dtype),
        in_specs=[vmem, vmem] + [hbm] * len(buffer),
        out_specs=hbm,
        scratch_shapes=[
            pltpu.VMEM(part.shape, part.dtype),
            pltpu.SemaphoreType.DMA((half,)),
        ],
        input_output_aliases={2: 0} if buffer else {},
        cost_estimate=pl.CostEstimate(
            flops=3 * part.size, bytes_accessed=12 * part.size, transcendentals=0
        ),
        compiler_params=pltpu.CompilerParams(vmem_limit_bytes=8 << 20),
        name="put_mine" if is_mine else "put_other",
    )(probe, part, *buffer)


def in_vmem(kernel, shapes, *operands):
    vmem = pl.BlockSpec(memory_space=pltpu.VMEM)
    out = tuple(jax.ShapeDtypeStruct(shape, jnp.float32) for shape in shapes)
    size = sum(a.size for a in out + operands)
    return pl.pallas_call(
        kernel,
        out_shape=out if len(out) > 1 else out[0],
        in_specs=[vmem] * len(operands),
        out_specs=(vmem,) * len(out) if len(out) > 1 else vmem,
        cost_estimate=pl.CostEstimate(flops=size, bytes_accessed=4 * size, transcendentals=0),
        compiler_params=pltpu.CompilerParams(vmem_limit_bytes=8 << 20),
    )(*operands)


def member_order(count):
    pairs = list(range(count // 2))
    order = []
    for at in pairs[0::2][::-1] + pairs[1::2][::-1]:
        order.extend((2 * at + 1, 2 * at))
    return order


def body(object_field, probe, patterns, offsets, counts):
    row_total = lax.axis_size("row")
    tile_total = row_total * lax.axis_size("col")
    modes, _, width, _ = probe.shape
    half = modes // 2

    pair = [(0, 1), (1, 0)]
    near = [(i, i ^ 1) for i in range(row_total)]
    far = [(i, i + 1) for i in range(1, row_total - 1, 2)]
    far = far + [(target, source) for source, target in far]

    near_block = lax.ppermute(object_field, "row", near)
    far_block = lax.ppermute(object_field, "row", far)
    own_pair = lax.ppermute(object_field, "col", pair)
    near_pair = lax.ppermute(near_block, "col", pair)
    far_pair = lax.ppermute(far_block, "col", pair)
    probe_here, patterns_here, own, tables, offsets, weight = stage(
        probe, patterns, object_field, jnp.asarray(host_tables(width)), offsets
    )
    blocks = (own, own_pair, near_block, near_pair, far_block, far_pair)
    send_probe, window, kept, part = run_first(
        offsets, counts, blocks, probe_here, patterns_here, tables
    )
    got_probe = lax.ppermute(send_probe, "col", pair)
    keep_probe, grads = run_second(offsets, probe_here, tables, window, kept, part)
    got_grad = lax.ppermute(grads[1], "col", pair)

    members = [member_order(row_total)]
    mine = (keep_probe + got_probe).reshape(row_total, -1, width)
    mine = lax.all_to_all(mine, "row", 0, 0, tiled=True, axis_index_groups=members)
    mine = in_vmem(total_kernel, [mine.shape], mine)
    block = own.shape
    middle, near_strip, far_strip = in_vmem(
        strips_kernel, [block, block, block], grads, got_grad
    )
    near_strip = lax.ppermute(near_strip, "row", near)
    far_strip = lax.ppermute(far_strip, "row", far)
    mine = lax.all_to_all(mine, "row", 0, 0, tiled=True, axis_index_groups=members)
    mine = mine.reshape(half, 2, width, width)
    other = lax.ppermute(mine, "col", pair)
    half_done = put_half(tile_total, True, probe_here, mine)
    object_field = in_vmem(
        object_kernel, [block], own, middle, near_strip, far_strip, weight
    )
    probe = put_half(tile_total, False, probe_here, other, half_done)
    return (object_field, probe)


def solution(mesh):
    placed = (
        P(None, ("tilt", "row"), "col"),
        P("tilt", None, None, None),
        P(("tilt", "row"), "col", None, None, None),
        P(("tilt", "row"), "col", None, None),
        P(("tilt", "row"), "col"),
    )

    return jax.shard_map(
        body,
        mesh=mesh,
        in_specs=placed,
        out_specs=(P(None, ("tilt", "row"), "col"), P("tilt", None, None, None)),
        check_vma=False,
    )
```
